32 devices in a mesh: rep: 4 (over y, x), fsdp: 4 (over z), tp: 2 (over core).
Axes of the slice: x: 2, y: 2, z: 4, core: 2. Of those that a mesh axis runs over, the one named last changes fastest.
Arguments:
- tokens: bfloat16 [4096, 8192], P(('rep', 'fsdp'), 'tp'), may hold values from -6 to 6
- cotangent: bfloat16 [4096, 512], P(('rep', 'fsdp'), 'tp'), may hold values from -6 to 6
- weight: bfloat16 [512, 8192], P('fsdp', 'tp'), may hold values from -0.0625 to 0.0625
- momentum: bfloat16 [4, 512, 8192], P('rep', 'fsdp', 'tp'), may hold values from -6 to 6
Outputs:
- projected: bfloat16 [4096, 512], P(('rep', 'fsdp'))
- update: float32 [512, 8192], P('fsdp', 'tp')
- momentum_out: float32 [4, 512, 8192], P('rep', 'fsdp', 'tp')
The draws below stay inside these ranges and needn't reach their ends.
All inputs are finite; a program needn't handle non-finite values.
Results may differ from the reference program's by a relative error of at most 0.006.
Values may be sent and summed in bfloat16 or wider, within the bound.
A program may use at most 64 MiB of HBM per device.

```python
import math
import jax
import jax.numpy as jnp
from jax import lax

D = 8192
COLS = 512
TOK_DEV = 256
TOKENS = 4096
N_REP = 4
N_FSDP = 4


def strengthened(array, key, source, target, shards_of, factor):
    def block_of(dim):
        return (jnp.arange(array.shape[dim]) // (array.shape[dim] // shards_of)).reshape((-1,) + (1,) * (array.ndim - 1 - dim))

    first = jax.random.permutation(key, shards_of)[block_of(target)]
    other_side = (block_of(target) + shards_of // 2) % shards_of
    return jnp.where((block_of(source) == first) | (block_of(source) == other_side), factor * array, array)


def levels(own_key, shape, split, low, largest):
    factor_of, own = 1.0, jax.random.fold_in(own_key, 6)
    for axis_at, shards_of in split:
        draws = jnp.exp(jax.random.uniform(jax.random.fold_in(own, axis_at), (shards_of,), jnp.float32, low / len(split), largest / len(split)))
        factor_of = factor_of * jnp.repeat(draws, shape[axis_at] // shards_of).reshape([-1 if axis == axis_at else 1 for axis in range(len(shape))])
    return factor_of


def scatter_about(stream_key, shape, width, most, shards=(), held_as=jnp.bfloat16):
    array = jax.random.normal(stream_key, shape, jnp.float32) * width
    if len(shards) > 0:
        array = levels(stream_key, shape, shards, -0.22, 0.18) * array
    return jnp.clip(array, min=-most, max=most).astype(held_as)


def heavy_noise(own_key, dims, spread, most, shards, heavy, dtype=jnp.bfloat16):
    entries = spread * jax.random.normal(own_key, dims, jnp.float32)
    if shards:
        entries = entries * levels(own_key, dims, shards, -0.22, 0.18)
    return jnp.clip(strengthened(entries, jax.random.fold_in(own_key, 3), *heavy), -most, most).astype(dtype)


def setup_inputs(seed: int = 0) -> dict:
    key_list = jax.random.split(jax.random.key(seed), 5)
    tokens = scatter_about(key_list[0], (TOKENS, D), 1.0, 6.0, ((0, 16), (1, 2)))
    cotangent = heavy_noise(key_list[1], (TOKENS, COLS), 1.0, 6.0, ((0, 16), (1, 2)), (0, 1, 16, 2.0))
    weight = scatter_about(key_list[2], (COLS, D), D ** -0.5, 0.0625, ((0, 4), (1, 2)))
    momentum = scatter_about(key_list[3], (N_REP, COLS, D), 1.0, 6.0, ((0, 4), (1, 4), (2, 2)))
    return dict(tokens=tokens, cotangent=cotangent, weight=weight, momentum=momentum)


BETA_ONE = 0.9
BETA_TWO = 0.99
SOFT_WIDTH = 0.25

def reference(tokens, cotangent, weight, momentum):
    projected = jnp.dot(tokens, weight.T, preferred_element_type=jnp.float32).astype(jnp.bfloat16)
    scale = 1.0 / math.sqrt(TOK_DEV * N_FSDP)
    token_blocks = tokens.reshape(N_REP, N_FSDP, TOK_DEV, D)
    cot_blocks = cotangent.reshape(N_REP, N_FSDP, TOK_DEV, COLS)

    def shard_term(running, inputs):
        rows, cots = inputs
        partial_term = jnp.dot(cots.T, rows, preferred_element_type=jnp.float32).astype(jnp.bfloat16)
        partial_term = lax.optimization_barrier(partial_term)
        return (running + partial_term.astype(jnp.float32), None)

    def replica(tally, inputs):
        rows, cots, moment_in = inputs
        gradient, _ = lax.scan(shard_term, jnp.zeros((COLS, D), jnp.float32), (rows, cots))
        gradient = gradient * scale
        moment = moment_in.astype(jnp.float32)
        blended = BETA_ONE * moment + (1.0 - BETA_ONE) * gradient
        soft_sign = jnp.clip(blended / SOFT_WIDTH, -1.0, 1.0)
        renewed = BETA_TWO * moment + (1.0 - BETA_TWO) * gradient
        return (tally + soft_sign, renewed)
    tally, momentum_out = lax.scan(replica, jnp.zeros((COLS, D), jnp.float32), (token_blocks, cot_blocks, momentum))
    update = jnp.clip(tally, -1.0, 1.0)
    return (projected, update, momentum_out)
```

```python
import functools
import math

import jax
import jax.numpy as jnp
from jax import lax
from jax.experimental import pallas as pl
from jax.experimental.pallas import tpu as pltpu
from jax.sharding import PartitionSpec as P

BETA_ONE = 0.9
BETA_TWO = 0.99
SOFT_WIDTH = 0.25
LANES = 128
WIDTH = 256
LAG = 3
WLAG = 2
PROJ_STEPS = 8
MESH = pl.DeviceIdType.MESH
F32 = jnp.float32
BF16 = jnp.bfloat16


def step(dims, scale, tok, cot, wgt, mom, proj, upd, grad, *scratch):
    (n, nrep, ntp, pieces, width, rows, low, chunks) = dims
    (tok_v, mom_v, part, right_buf, left_buf, weights, cots, edge_cots, cots_t, edge_cots_t, edge_toks,
     halves, edge_out, edge_in, ones, pairs) = scratch[:16]
    (loc, cs, cr, es, er, fs, fr, ks, kr, rs_s, rs_r, ls_s, ls_r, wrs, wrr, wls, wlr, wps, wpr,
     hs, hr, os, orr, vs, vr, ts, tr) = scratch[16:]
    z, me, t = lax.axis_index("fsdp"), lax.axis_index("rep"), lax.axis_index("tp")
    high = nrep // low
    tp_cols = cot.shape[1]
    held = tok.shape[0]
    share = wgt.shape[1] // (nrep * chunks)
    inner = (z > 0) & (z < n - 1)
    beside = (z == 1) | (z == n - 2)
    own_rows = pl.ds(pl.multiple_of(z * rows, rows), rows)

    def to(axis, at):
        return dict(device_id={axis: at}, device_id_type=MESH)

    def cols(p):
        return pl.ds(pl.multiple_of(p * width, LANES), width)

    def cot_copy(off):
        return pltpu.make_async_remote_copy(
            cot, cots.at[t], cs.at[off], cr.at[off], **to("tp", lax.rem(t + off, ntp)))

    def edge_cot(target):
        return pltpu.make_async_remote_copy(cot, edge_cots.at[t], es.at[0], er.at[0], **to("fsdp", target))

    def edge_cot_relay(off):
        return pltpu.make_async_remote_copy(
            edge_cots.at[t], edge_cots.at[t], fs.at[off], fr.at[off], **to("tp", lax.rem(t + off, ntp)))

    def edge_tok(p, target):
        return pltpu.make_async_remote_copy(
            tok.at[:, cols(p)], edge_toks.at[p], ks.at[p], kr.at[p], **to("fsdp", target))

    def sum_copy(buf, p, k, send, recv, target):
        slot = buf.at[p, pl.ds(pl.multiple_of(k * rows, rows), rows), :]
        return pltpu.make_async_remote_copy(slot, slot, send.at[p, k], recv.at[p, k], **to("fsdp", target))

    def weight_cols(c):
        return pl.ds(pl.multiple_of((me * chunks + c) * share, LANES), share)

    def weight_slot(shard, c):
        return weights.at[pl.ds(pl.multiple_of(shard * rows, rows), rows), weight_cols(c)]

    def weight_line(own, shard, c, send, recv, target):
        slot = weight_slot(shard, c)
        source = wgt.at[:, weight_cols(c)] if own else slot
        return pltpu.make_async_remote_copy(
            source, slot, send.at[shard, c], recv.at[shard, c], **to("fsdp", target))

    def weight_plane(shard, c, off):
        slot = weight_slot(shard, c)
        return pltpu.make_async_remote_copy(
            slot, slot, wps.at[shard, c, off], wpr.at[shard, c, off], **to("rep", lax.rem(me + off, nrep)))

    def half_copy(off):
        return pltpu.make_async_remote_copy(
            halves.at[t], halves.at[t], hs.at[off], hr.at[off], **to("tp", lax.rem(t + off, ntp)))

    def out_copy(target):
        return pltpu.make_async_remote_copy(edge_out, edge_in, os.at[0], orr.at[0], **to("fsdp", target))

    def group(stage, p):
        mine, rest = lax.rem(me, low), me // low
        turn = lax.rem(p, 2) if low == high else 0
        along = turn if stage == 0 else 1 - turn
        size = (low, high)[stage]
        at = (1 - along) * mine + along * rest

        def peer(off):
            pos = lax.rem(at + off, size)
            return (1 - along) * (rest * low + pos) + along * (pos * low + mine)

        return size, at, peer

    def vote_copy(stage, p, off):
        _, at, peer = group(stage, p)
        slot = (ones, pairs)[stage].at[p, at]
        send, recv = ((vs, vr), (ts, tr))[stage]
        return pltpu.make_async_remote_copy(slot, slot, send.at[p, off], recv.at[p, off], **to("rep", peer(off)))

    def turned(source, target):
        for b in range(ntp):
            target[b * tp_cols:(b + 1) * tp_cols, :] = source[b].T

    def weight_step(s):
        for h in range(1, n - 1):
            for send, recv, shard, target, edge in (
                (wrs, wrr, z - h, z + 1, z - h == 0), (wls, wlr, z + h, z - 1, z + h == n - 1)):
                c = s - WLAG * (h - 1) - jnp.where(edge, 2, 0)
                on = (target > 0) & (target < n - 1)

                @pl.when(inner & (shard >= 0) & (shard < n) & (c >= 0) & (c < chunks))
                def _():
                    weight_line(False, shard, c, send, recv, z).wait_recv()

                    @pl.when(on)
                    def _():
                        weight_line(False, shard, c, send, recv, target).start()

                    for off in range(1, nrep):
                        weight_plane(shard, c, off).start()

    def token_step(s):
        @pl.when(beside & (s < pieces))
        def _():
            @pl.when(s == 0)
            def _():
                edge_cot(z).wait_recv()
                for off in range(1, ntp):
                    edge_cot_relay(off).start()
                for off in range(1, ntp):
                    edge_cot_relay(off).wait_recv()
                turned(edge_cots, edge_cots_t)

            edge_tok(s, z).wait_recv()
            total = jnp.dot(edge_cots_t[...], edge_toks[s], preferred_element_type=F32) + part[s].astype(F32)

            @pl.when(z == 1)
            def _():
                right_buf[s] = total.astype(BF16)

            @pl.when(z == n - 2)
            def _():
                left_buf[s] = total.astype(BF16)

    flows = ((right_buf, rs_s, rs_r, 1, z), (left_buf, ls_s, ls_r, -1, n - 1 - z))

    def sum_step(s):
        for first in (True, False):
            for j in range(n - 2, 0, -1):
                p = s - LAG * (n - 2 - j)
                for buf, send, recv, way, depth in flows:
                    k = z + way * j
                    ok = (p >= 0) & (p < pieces) & (k >= 0) & (k < n)

                    @pl.when(ok & ((depth == 1) if first else (depth > 1)))
                    def _():
                        if not first:
                            rk = pl.ds(pl.multiple_of(k * rows, rows), rows)
                            sum_copy(buf, p, k, send, recv, z).wait_recv()
                            buf[p, rk, :] = (buf[p, rk, :].astype(F32) + part[p, rk, :].astype(F32)).astype(BF16)
                        sum_copy(buf, p, k, send, recv, z + way).start()

    def vote(p):
        for buf, send, recv, way, depth in flows:
            @pl.when(depth > 1)
            def _():
                sum_copy(buf, p, z, send, recv, z).wait_recv()
        keep = jnp.where(beside, 0.0, 1.0).astype(F32)
        g = (part[p, own_rows, :].astype(F32) * keep + right_buf[p, own_rows, :].astype(F32)
             + left_buf[p, own_rows, :].astype(F32)) * scale
        grad[:, cols(p)] = g.astype(BF16)
        blended = BETA_ONE * mom_v[:, cols(p)].astype(F32) + (1.0 - BETA_ONE) * g
        size, at, _ = group(0, p)
        ones[p, at] = jnp.clip(blended / SOFT_WIDTH, -1.0, 1.0).astype(BF16)
        for off in range(1, size):
            vote_copy(0, p, off).start()

    def added(stage, p):
        size, at, _ = group(stage, p)
        for off in range(1, size):
            vote_copy(stage, p, off).wait_recv()
        buf = (ones, pairs)[stage]
        total = buf[p, 0].astype(F32)
        for i in range(1, size):
            total = total + buf[p, i].astype(F32)
        return total

    def count(p):
        total = added(0, p)
        size, at, _ = group(1, p)
        pairs[p, at] = total.astype(BF16)
        for off in range(1, size):
            vote_copy(1, p, off).start()

    def finish(p):
        upd[:, cols(p)] = jnp.clip(added(1, p), -1.0, 1.0).astype(BF16)
        for stage in range(2):
            for off in range(1, group(stage, p)[0]):
                vote_copy(stage, p, off).wait_send()
        for j in range(1, n - 1):
            for buf, send, recv, way, depth in flows:
                k = z + way * j

                @pl.when((depth > 0) & (k >= 0) & (k < n))
                def _():
                    sum_copy(buf, p, k, send, recv, z).wait_send()

        @pl.when((z == 0) | (z == n - 1))
        def _():
            edge_tok(p, z).wait_send()

    first_proj = 2 + chunks + WLAG * (n - 3) + 3
    per = -(-pieces // PROJ_STEPS)

    def project(s):
        @pl.when(inner & (s == first_proj))
        def _():
            for shard in range(n):
                @pl.when(shard != z)
                def _():
                    @pl.loop(0, chunks)
                    def _(c):
                        for off in range(1, nrep):
                            weight_plane(shard, c, off).wait_recv()
            halves[t] = jnp.zeros(halves.shape[1:], F32)

        @pl.when(inner & (s >= first_proj) & (s < first_proj + PROJ_STEPS))
        def _():
            for i in range(per):
                p = (s - first_proj) * per + i

                @pl.when(p < pieces)
                def _():
                    w = weights[:, cols(p)]
                    halves[t, 0] += lax.dot_general(
                        tok_v[:, cols(p)], w, (((1,), (1,)), ((), ())), preferred_element_type=F32)

                    @pl.when(beside)
                    def _():
                        halves[t, 1] += lax.dot_general(
                            edge_toks[p], w, (((1,), (1,)), ((), ())), preferred_element_type=F32)

        @pl.when(inner & (s == first_proj + PROJ_STEPS))
        def _():
            for off in range(1, ntp):
                half_copy(off).start()

        @pl.when(inner & (s == first_proj + PROJ_STEPS + 1))
        def _():
            for off in range(1, ntp):
                half_copy(off).wait_recv()
            for which, target in ((0, proj), (1, edge_out)):
                total = halves[0, which]
                for b in range(1, ntp):
                    total = total + halves[b, which]
                target[...] = total.astype(BF16)

            @pl.when(z == 1)
            def _():
                out_copy(z - 1).start()

            @pl.when(z == n - 2)
            def _():
                out_copy(z + 1).start()

            for off in range(1, ntp):
                half_copy(off).wait_send()
            for shard in range(n):
                @pl.when(shard != z)
                def _():
                    @pl.loop(0, chunks)
                    def _(c):
                        for off in range(1, nrep):
                            weight_plane(shard, c, off).wait_send()

    tok_load = pltpu.make_async_copy(tok, tok_v, loc.at[0])
    mom_load = pltpu.make_async_copy(mom.at[0], mom_v, loc.at[1])
    cot_load = pltpu.make_async_copy(cot, cots.at[t], loc.at[2])
    wgt_load = pltpu.make_async_copy(wgt, weights.at[own_rows, :], loc.at[3])
    barrier = pltpu.get_barrier_semaphore()
    for axis, at, size in (("tp", t, ntp), ("rep", me, nrep)):
        for off in range(1, size):
            pl.semaphore_signal(barrier, inc=1, **to(axis, lax.rem(at + off, size)))

    @pl.when(z > 0)
    def _():
        pl.semaphore_signal(barrier, inc=1, **to("fsdp", z - 1))

    @pl.when(z < n - 1)
    def _():
        pl.semaphore_signal(barrier, inc=1, **to("fsdp", z + 1))

    cot_load.start()
    tok_load.start()
    wgt_load.start()
    mom_load.start()
    pl.semaphore_wait(barrier, ntp + nrep - 2 + jnp.where(inner, 2, 1))

    for edge, target, send, recv in ((0, z + 1, wrs, wrr), (n - 1, z - 1, wls, wlr)):
        @pl.when(z == edge)
        def _():
            edge_cot(target).start()
            for p in range(2):
                edge_tok(p, target).start()

    for off in range(1, ntp):
        cot_copy(off).start()

    for send, recv, target in ((wrs, wrr, z + 1), (wls, wlr, z - 1)):
        @pl.when(inner & (target > 0) & (target < n - 1))
        def _():
            @pl.loop(0, chunks)
            def _(c):
                weight_line(True, z, c, send, recv, target).start()

    for edge, target, send, recv in ((0, z + 1, wrs, wrr), (n - 1, z - 1, wls, wlr)):
        @pl.when(z == edge)
        def _():
            @pl.loop(2, pieces)
            def _(p):
                @pl.when(p - 2 < chunks)
                def _():
                    weight_line(True, z, p - 2, send, recv, target).start()

                edge_tok(p, target).start()

    for buf, edge in ((right_buf, 0), (left_buf, n - 1)):
        @pl.when(z == edge)
        def _():
            buf[:, edge * rows:(edge + 1) * rows, :] = jnp.zeros((pieces, rows, width), BF16)
    cot_load.wait()
    for off in range(1, ntp):
        cot_copy(off).wait_recv()
    turned(cots, cots_t)
    tok_load.wait()

    @pl.loop(0, pieces)
    def _(p):
        part[p] = jnp.dot(cots_t[...], tok_v[:, cols(p)], preferred_element_type=F32).astype(BF16)

    wgt_load.wait()
    mom_load.wait()

    voting = LAG * (n - 2)
    last = max(pieces + voting + 4, first_proj + PROJ_STEPS + 2)

    @pl.loop(0, last)
    def _(s):
        weight_step(s)
        token_step(s)
        sum_step(s)
        for work, at in ((vote, voting), (count, voting + 2), (finish, voting + 4)):
            @pl.when((s >= at) & (s < at + pieces))
            def _():
                work(s - at)
        project(s)

    for edge, target, send, recv in ((0, z + 1, wrs, wrr), (n - 1, z - 1, wls, wlr)):
        @pl.when(z == edge)
        def _():
            out_copy(target).wait_recv()
            proj[...] = edge_in[...]
            edge_cot(target).wait_send()

            @pl.loop(0, chunks)
            def _(c):
                weight_line(True, z, c, send, recv, target).wait_send()

    for off in range(1, ntp):
        cot_copy(off).wait_send()

    @pl.when(beside)
    def _():
        for off in range(1, ntp):
            edge_cot_relay(off).wait_send()
        out_copy(z).wait_send()

    for shard in range(n):
        for send, recv, target, ok in ((wrs, wrr, z + 1, shard <= z), (wls, wlr, z - 1, shard >= z)):
            @pl.when(inner & ok & (target > 0) & (target < n - 1))
            def _():
                @pl.loop(0, chunks)
                def _(c):
                    weight_line(False, shard, c, send, recv, target).wait_send()


def shards(n, nrep, ntp, tokens, cotangent, weight, momentum):
    held, half = tokens.shape
    rows, cols = weight.shape[0], weight.shape[0] * n
    width = min(WIDTH, half)
    pieces = half // width
    low = max(r for r in range(1, nrep + 1) if nrep % r == 0 and r * r <= nrep)
    chunks = max(1, min(4, half // (nrep * LANES)))
    most = max(low, nrep // low)
    scale = 1.0 / math.sqrt(held * n)
    dma = pltpu.SemaphoreType.DMA
    vmem = pl.BlockSpec(memory_space=pltpu.VMEM)
    hbm = pl.BlockSpec(memory_space=pltpu.HBM)
    projected, update, gradient = pl.pallas_call(
        functools.partial(step, (n, nrep, ntp, pieces, width, rows, low, chunks), scale),
        out_shape=(
            jax.ShapeDtypeStruct((held, cols), BF16),
            jax.ShapeDtypeStruct((rows, half), BF16),
            jax.ShapeDtypeStruct((rows, half), BF16),
        ),
        in_specs=[hbm] * 4,
        out_specs=(vmem,) * 3,
        scratch_shapes=[
            pltpu.VMEM((held, half), BF16),
            pltpu.VMEM((rows, half), BF16),
            pltpu.VMEM((pieces, cols, width), BF16),
            pltpu.VMEM((pieces, cols, width), BF16),
            pltpu.VMEM((pieces, cols, width), BF16),
            pltpu.VMEM((cols, half), BF16),
            pltpu.VMEM((ntp,) + cotangent.shape, BF16),
            pltpu.VMEM((ntp,) + cotangent.shape, BF16),
            pltpu.VMEM((cols, held), BF16),
            pltpu.VMEM((cols, held), BF16),
            pltpu.VMEM((pieces, held, width), BF16),
            pltpu.VMEM((ntp, 2, held, cols), F32),
            pltpu.VMEM((held, cols), BF16),
            pltpu.VMEM((held, cols), BF16),
            pltpu.VMEM((pieces, most, rows, width), BF16),
            pltpu.VMEM((pieces, most, rows, width), BF16),
        ]
        + [dma((4,))]
        + [dma((ntp,))] * 2
        + [dma((1,))] * 2
        + [dma((ntp,))] * 2
        + [dma((pieces,))] * 2
        + [dma((pieces, n))] * 4
        + [dma((n, chunks))] * 4
        + [dma((n, chunks, nrep))] * 2
        + [dma((ntp,))] * 2
        + [dma((1,))] * 2
        + [dma((pieces, most))] * 4,
        compiler_params=pltpu.CompilerParams(
            collective_id=0, has_side_effects=True, vmem_limit_bytes=44 * 1024 * 1024
        ),
    )(tokens, cotangent, weight, momentum)
    renewed = BETA_TWO * momentum.astype(F32) + (1.0 - BETA_TWO) * gradient.astype(F32)[None]
    return (projected, update.astype(F32), renewed)


def solution(mesh):
    sizes = dict(mesh.shape)
    return jax.shard_map(
        functools.partial(shards, sizes["fsdp"], sizes["rep"], sizes["tp"]),
        mesh=mesh,
        in_specs=(
            P(("rep", "fsdp"), "tp"),
            P(("rep", "fsdp"), "tp"),
            P("fsdp", "tp"),
            P("rep", "fsdp", "tp"),
        ),
        out_specs=(P(("rep", "fsdp"), None), P("fsdp", "tp"), P("rep", "fsdp", "tp")),
        check_vma=False,
    )
```

```python
import functools
import math

import jax
import jax.numpy as jnp
from jax import lax
from jax.experimental import pallas as pl
from jax.experimental.pallas import tpu as pltpu
from jax.sharding import PartitionSpec as P

BETA_ONE = 0.9
BETA_TWO = 0.99
SOFT_WIDTH = 0.25
LANES = 128
WIDTH = 256
LAG = 3
HOLD = 1
BURST = 2
WLAG = 2
RELAY = 3
COUNT = 4
FINISH = 4
PROJ_STEPS = 8
MESH = pl.DeviceIdType.MESH
F32 = jnp.float32
BF16 = jnp.bfloat16


def step(dims, scale, tok, cot, wgt, mom, proj, upd, grad, *scratch):
    (n, nrep, ntp, pieces, width, rows, low, chunks) = dims
    (tok_v, mom_v, part, right_buf, left_buf, weights, cots, edge_cots, cots_t, edge_cots_t, edge_toks,
     halves, edge_half, edge_got, edge_out, edge_in, proj_v, upd_v, grad_v, ones, pairs) = scratch[:21]
    (loc, cs, cr, es, er, fs, fr, ks, kr, rs_s, rs_r, ls_s, ls_r, wrs, wrr, wls, wlr, wps, wpr, wqs,
     hs, hr, gs, gr, os, orr, qs, qr, vs, vr, ts, tr, us, ds) = scratch[21:]
    held_rows = tok.shape[0]
    z, me, t = lax.axis_index("fsdp"), lax.axis_index("rep"), lax.axis_index("tp")
    high = nrep // low
    split = ones.shape[0] // pieces
    part_width = width // split
    band = held_rows // ntp
    tp_cols = cot.shape[1]
    share = wgt.shape[1] // (nrep * chunks)
    inner = (z > 0) & (z < n - 1)
    beside = (z == 1) | (z == n - 2)
    own_rows = pl.ds(pl.multiple_of(z * rows, rows), rows)

    def to(axis, at):
        return dict(device_id={axis: at}, device_id_type=MESH)

    def cols(p):
        return pl.ds(pl.multiple_of(p * width, LANES), width)

    flows = ((right_buf, rs_s, rs_r, 1, z), (left_buf, ls_s, ls_r, -1, n - 1 - z))

    def cot_copy(off):
        return pltpu.make_async_remote_copy(
            cot, cots.at[t], cs.at[off - 1], cr.at[off - 1], **to("tp", lax.rem(t + off, ntp)))

    def edge_cot(target):
        return pltpu.make_async_remote_copy(cot, edge_cots.at[t], es.at[0], er.at[0], **to("fsdp", target))

    def edge_cot_relay(off):
        return pltpu.make_async_remote_copy(
            edge_cots.at[t], edge_cots.at[t], fs.at[off - 1], fr.at[off - 1], **to("tp", lax.rem(t + off, ntp)))

    def edge_tok(p, target):
        return pltpu.make_async_remote_copy(
            tok.at[:, cols(p)], edge_toks.at[p], ks.at[0], kr.at[p], **to("fsdp", target))

    def sum_copy(flow, p, k, sent=True):
        buf, send, recv, way, _ = flow
        slot = buf.at[p, pl.ds(pl.multiple_of(k * rows, rows), rows), :]
        hop = (k - z) * way
        return pltpu.make_async_remote_copy(
            slot, slot, send.at[k], recv.at[p, hop - 1 if sent else hop], **to("fsdp", z + way if sent else z))

    def sums_sent(flow, k):
        buf, send, recv, way, _ = flow
        slot = buf.at[:, pl.ds(pl.multiple_of(k * rows, rows), rows), :]
        return pltpu.make_async_remote_copy(slot, slot, send.at[k], recv.at[0, 0], **to("fsdp", z))

    def weight_cols(c):
        return pl.ds(pl.multiple_of((me * chunks + c) * share, LANES), share)

    def weight_slot(shard, c):
        return weights.at[pl.ds(pl.multiple_of(shard * rows, rows), rows), weight_cols(c)]

    def weight_line(own, shard, c, send, recv, target):
        slot = weight_slot(shard, c)
        source = wgt.at[:, weight_cols(c)] if own else slot
        return pltpu.make_async_remote_copy(
            source, slot, send.at[shard], recv.at[shard, c], **to("fsdp", target))

    def line_sent(shard, send):
        slot = plane_slot(shard, me)
        return pltpu.make_async_remote_copy(slot, slot, send.at[shard], wrr.at[shard, 0], **to("fsdp", z))

    mine, rest = lax.rem(me, low), me // low
    sizes = (low, high)

    def beside_me(way, off):
        if way == 0:
            return rest * low + lax.rem(mine + off, low)
        return lax.rem(rest + off, high) * low + mine

    def before_me(way, off):
        if way == 0:
            return rest * low + lax.rem(mine + low - off, low)
        return lax.rem(rest + high - off, high) * low + mine

    def plane_slot(shard, source, lo=0, hi=None):
        hi = chunks if hi is None else hi
        return weights.at[pl.ds(pl.multiple_of(shard * rows, rows), rows),
                          pl.ds(pl.multiple_of((source * chunks + lo) * share, LANES), (hi - lo) * share)]

    def plane_bytes(count):
        return weights.at[0:(n - 1) * rows, 0:count * share]

    def weight_plane(shard, way, off):
        slot = plane_slot(shard, me)
        return pltpu.make_async_remote_copy(
            slot, slot, wps.at[way, off - 1], wpr.at[shard, me], **to("rep", beside_me(way, off)))

    cut = (chunks + 1) // 2
    cuts = ((0, cut), (cut, chunks))

    def weight_relay(shard, way, off, onward):
        source = before_me(way, off)
        slot = plane_slot(shard, source, *cuts[way])
        return pltpu.make_async_remote_copy(
            slot, slot, wqs.at[way, (off - 1) * max(sizes) + onward - 1], wpr.at[shard, source],
            **to("rep", beside_me(1 - way, onward)))

    def weight_from(shard, source):
        slot = plane_slot(shard, source)
        return pltpu.make_async_remote_copy(
            slot, slot, wps.at[0, 0], wpr.at[shard, source], **to("rep", source))

    def plane_sent(sem, count):
        return pltpu.make_async_remote_copy(
            plane_bytes(count), plane_bytes(count), sem, wpr.at[0, 0], **to("rep", me))

    def half_copy(off):
        return pltpu.make_async_remote_copy(
            halves.at[t], halves.at[t], hs.at[off - 1], hr.at[off - 1], **to("tp", lax.rem(t + off, ntp)))

    def edge_half_copy(off):
        other = lax.rem(t + off, ntp)
        return pltpu.make_async_remote_copy(
            edge_half.at[pl.ds(pl.multiple_of(other * band, band), band), :], edge_got.at[t],
            gs.at[off - 1], gr.at[off - 1], **to("tp", other))

    def out_copy(target):
        return pltpu.make_async_remote_copy(edge_out, edge_in.at[t], os.at[0], orr.at[0], **to("fsdp", target))

    def out_relay(off):
        return pltpu.make_async_remote_copy(
            edge_in.at[t], edge_in.at[t], qs.at[off - 1], qr.at[off - 1], **to("tp", lax.rem(t + off, ntp)))

    def grad_out(p):
        return pltpu.make_async_copy(grad_v.at[p], grad.at[:, cols(p)], ds.at[0])

    def upd_out(p):
        return pltpu.make_async_copy(upd_v.at[p], upd.at[:, cols(p)], us.at[0])

    proj_out = pltpu.make_async_copy(proj_v, proj, loc.at[4])

    def group(stage, i):
        turn = lax.rem(i, 2) if low == high else 0
        along = turn if stage == 0 else 1 - turn
        size = sizes[stage]
        at = (1 - along) * mine + along * rest

        def peer(off):
            pos = lax.rem(at + off, size)
            return (1 - along) * (rest * low + pos) + along * (pos * low + mine)

        return size, at, peer

    def vote_copy(stage, i, off):
        _, at, peer = group(stage, i)
        slot = (ones, pairs)[stage].at[i, at]
        send, recv = ((vs, vr), (ts, tr))[stage]
        return pltpu.make_async_remote_copy(slot, slot, send.at[off - 1], recv.at[i, off - 1], **to("rep", peer(off)))

    def turned(source, target):
        for b in range(ntp):
            target[b * tp_cols:(b + 1) * tp_cols, :] = source[b].T

    def weight_step(s):
        for h in range(1, n - 1):
            for send, recv, shard, target, edge in (
                (wrs, wrr, z - h, z + 1, z - h == 0), (wls, wlr, z + h, z - 1, z + h == n - 1)):
                at = WLAG * (h - 1) + jnp.where(edge, BURST, 0)
                on = (target > 0) & (target < n - 1)
                here = inner & (shard >= 0) & (shard < n)

                @pl.when(here & (s == at))
                def _():
                    @pl.loop(0, chunks)
                    def _(c):
                        weight_line(False, shard, c, send, recv, z).wait_recv()

                        @pl.when(on)
                        def _():
                            weight_line(False, shard, c, send, recv, target).start()

                    for way in range(2):
                        for off in range(1, sizes[way]):
                            weight_plane(shard, way, off).start()

                @pl.when(here & (s == at + RELAY))
                def _():
                    for way in range(2):
                        for off in range(1, sizes[way]):
                            weight_from(shard, before_me(way, off)).wait_recv()
                            if cuts[way][0] < cuts[way][1]:
                                for onward in range(1, sizes[1 - way]):
                                    weight_relay(shard, way, off, onward).start()

    def weights_ready(shard):
        for a in range(1, low):
            for b in range(1, high):
                source = lax.rem(rest + high - b, high) * low + lax.rem(mine + low - a, low)
                weight_from(shard, source).wait_recv()

    def weights_sent():
        for way in range(2):
            for off in range(1, sizes[way]):
                plane_sent(wps.at[way, off - 1], chunks).wait_send()
                if cuts[way][0] < cuts[way][1]:
                    for onward in range(1, sizes[1 - way]):
                        plane_sent(wqs.at[way, (off - 1) * max(sizes) + onward - 1],
                                   cuts[way][1] - cuts[way][0]).wait_send()

    def token_step(s):
        @pl.when(beside & (s < pieces))
        def _():
            @pl.when(s == 0)
            def _():
                edge_cot(z).wait_recv()
                for off in range(1, ntp):
                    edge_cot_relay(off).start()
                for off in range(1, ntp):
                    edge_cot_relay(off).wait_recv()
                turned(edge_cots, edge_cots_t)

            edge_tok(s, z).wait_recv()
            total = jnp.dot(edge_cots_t[...], edge_toks[s], preferred_element_type=F32) + part[s].astype(F32)

            @pl.when(z == 1)
            def _():
                right_buf[s] = total.astype(BF16)

            @pl.when(z == n - 2)
            def _():
                left_buf[s] = total.astype(BF16)

    def sum_step(s):
        for first in (True, False):
            for j in range(n - 2, 0, -1):
                for flow in flows:
                    buf, _, _, way, depth = flow
                    p = s - LAG * (depth - 1) - HOLD * (n - 1 - depth - j)
                    k = z + way * j
                    ok = (p >= 0) & (p < pieces) & (k >= 0) & (k < n)

                    @pl.when(ok & ((depth == 1) if first else (depth > 1)))
                    def _():
                        if not first:
                            rk = pl.ds(pl.multiple_of(k * rows, rows), rows)
                            sum_copy(flow, p, k, False).wait_recv()
                            buf[p, rk, :] = (buf[p, rk, :].astype(F32) + part[p, rk, :].astype(F32)).astype(BF16)
                        sum_copy(flow, p, k).start()

    def vote(p):
        for flow in flows:
            @pl.when(flow[4] > 1)
            def _():
                sum_copy(flow, p, z, False).wait_recv()
        keep = jnp.where(beside, 0.0, 1.0).astype(F32)
        for q in range(split):
            i = p * split + q
            cut = slice(q * part_width, (q + 1) * part_width)
            at = pl.ds(pl.multiple_of(i * part_width, LANES), part_width)
            g = (part[p, own_rows, cut].astype(F32) * keep + right_buf[p, own_rows, cut].astype(F32)
                 + left_buf[p, own_rows, cut].astype(F32)) * scale
            grad_v[p, :, cut] = g.astype(BF16)
            blended = BETA_ONE * mom_v[:, at].astype(F32) + (1.0 - BETA_ONE) * g
            size, place, _ = group(0, i)
            ones[i, place] = jnp.clip(blended / SOFT_WIDTH, -1.0, 1.0).astype(BF16)
            for off in range(1, size):
                vote_copy(0, i, off).start()
        grad_out(p).start()

    def added(stage, i):
        size, place, _ = group(stage, i)
        for off in range(1, size):
            vote_copy(stage, i, off).wait_recv()
        buf = (ones, pairs)[stage]
        total = buf[i, 0].astype(F32)
        for b in range(1, size):
            total = total + buf[i, b].astype(F32)
        return total

    def count(p):
        for q in range(split):
            i = p * split + q
            total = added(0, i)
            size, place, _ = group(1, i)
            pairs[i, place] = total.astype(BF16)
            for off in range(1, size):
                vote_copy(1, i, off).start()

    def finish(p):
        for q in range(split):
            upd_v[p, :, q * part_width:(q + 1) * part_width] = jnp.clip(
                added(1, p * split + q), -1.0, 1.0).astype(BF16)
        upd_out(p).start()

    first_proj = max(BURST + WLAG * (n - 3), WLAG * (n - 2)) + RELAY + 2
    per = -(-pieces // PROJ_STEPS)
    speed = 3
    first_edge = min(first_proj, pieces - -(-pieces // speed))

    def product(p, toks):
        return lax.dot_general(
            toks, weights[:, cols(p)], (((1,), (1,)), ((), ())), preferred_element_type=F32)

    def project(s):
        @pl.when(inner & (s == first_edge))
        def _():
            for shard in range(n):
                @pl.when(shard != z)
                def _():
                    weights_ready(shard)
            halves[t] = jnp.zeros(halves.shape[1:], F32)
            edge_half[...] = jnp.zeros(edge_half.shape, F32)

        @pl.when(beside & (s >= first_edge) & (s < pieces))
        def _():
            @pl.loop(jnp.minimum(s, speed * (s - first_edge)), jnp.minimum(s + 1, speed * (s - first_edge + 1)))
            def _(p):
                edge_half[...] += product(p, edge_toks[p])

            @pl.when(s == pieces - 1)
            def _():
                for off in range(1, ntp):
                    edge_half_copy(off).start()

        @pl.when(beside & (s == pieces))
        def _():
            total = edge_half[pl.ds(pl.multiple_of(t * band, band), band), :]
            for off in range(1, ntp):
                edge_half_copy(off).wait_recv()
            for off in range(1, ntp):
                total = total + edge_got[lax.rem(t + off, ntp)]
            edge_out[...] = total.astype(BF16)

            @pl.when(z == 1)
            def _():
                out_copy(z - 1).start()

            @pl.when(z == n - 2)
            def _():
                out_copy(z + 1).start()

        @pl.when(inner & (s >= first_proj) & (s < first_proj + PROJ_STEPS))
        def _():
            for i in range(per):
                p = (s - first_proj) * per + i

                @pl.when(p < pieces)
                def _():
                    halves[t] += product(p, tok_v[:, cols(p)])

        @pl.when(inner & (s == first_proj + PROJ_STEPS))
        def _():
            for off in range(1, ntp):
                half_copy(off).start()

        @pl.when(inner & (s == first_proj + PROJ_STEPS + 1))
        def _():
            for off in range(1, ntp):
                half_copy(off).wait_recv()
            total = halves[0]
            for b in range(1, ntp):
                total = total + halves[b]
            proj_v[...] = total.astype(BF16)
            proj_out.start()
            for off in range(1, ntp):
                half_copy(off).wait_send()
            weights_sent()

    tok_load = pltpu.make_async_copy(tok, tok_v, loc.at[0])
    mom_load = pltpu.make_async_copy(mom.at[0], mom_v, loc.at[1])
    cot_load = pltpu.make_async_copy(cot, cots.at[t], loc.at[2])
    wgt_load = pltpu.make_async_copy(wgt, weights.at[own_rows, :], loc.at[3])
    barrier = pltpu.get_barrier_semaphore()
    for axis, at, size in (("tp", t, ntp), ("rep", me, nrep)):
        for off in range(1, size):
            pl.semaphore_signal(barrier, inc=1, **to(axis, lax.rem(at + off, size)))

    @pl.when(z > 0)
    def _():
        pl.semaphore_signal(barrier, inc=1, **to("fsdp", z - 1))

    @pl.when(z < n - 1)
    def _():
        pl.semaphore_signal(barrier, inc=1, **to("fsdp", z + 1))

    cot_load.start()
    tok_load.start()
    wgt_load.start()
    mom_load.start()
    pl.semaphore_wait(barrier, ntp + nrep - 2 + jnp.where(inner, 2, 1))

    for edge, target, send, recv in ((0, z + 1, wrs, wrr), (n - 1, z - 1, wls, wlr)):
        @pl.when(z == edge)
        def _():
            edge_cot(target).start()
            for p in range(BURST):
                edge_tok(p, target).start()

    for off in range(1, ntp):
        cot_copy(off).start()

    for send, recv, target in ((wrs, wrr, z + 1), (wls, wlr, z - 1)):
        @pl.when(inner & (target > 0) & (target < n - 1))
        def _():
            @pl.loop(0, chunks)
            def _(c):
                weight_line(True, z, c, send, recv, target).start()

    for edge, target, send, recv in ((0, z + 1, wrs, wrr), (n - 1, z - 1, wls, wlr)):
        @pl.when(z == edge)
        def _():
            @pl.loop(0, chunks)
            def _(c):
                weight_line(True, z, c, send, recv, target).start()

            @pl.loop(BURST, pieces)
            def _(p):
                edge_tok(p, target).start()

    for buf, edge in ((right_buf, 0), (left_buf, n - 1)):
        @pl.when(z == edge)
        def _():
            buf[:, edge * rows:(edge + 1) * rows, :] = jnp.zeros((pieces, rows, width), BF16)
    cot_load.wait()
    for off in range(1, ntp):
        cot_copy(off).wait_recv()
    turned(cots, cots_t)
    tok_load.wait()

    @pl.loop(0, pieces)
    def _(p):
        part[p] = jnp.dot(cots_t[...], tok_v[:, cols(p)], preferred_element_type=F32).astype(BF16)

    wgt_load.wait()
    mom_load.wait()

    deep = jnp.maximum(z, n - 1 - z)
    voting = LAG * (deep - 1) + HOLD * (n - 1 - deep)
    last = max(pieces + LAG * (n - 2), first_proj + PROJ_STEPS + 2)

    @pl.loop(0, last)
    def _(s):
        weight_step(s)
        token_step(s)
        sum_step(s)
        for work, at in ((vote, voting), (count, voting + COUNT), (finish, voting + COUNT + FINISH)):
            @pl.when((s >= at) & (s < at + pieces))
            def _():
                work(s - at)
        project(s)

    @pl.loop(jnp.minimum(last - voting - COUNT, pieces), pieces)
    def _(p):
        count(p)

    for edge, target, send, recv in ((0, z + 1, wrs, wrr), (n - 1, z - 1, wls, wlr)):
        @pl.when(z == edge)
        def _():
            out_copy(target).wait_recv()
            for off in range(1, ntp):
                out_relay(off).start()
            edge_cot(target).wait_send()

            line_sent(z, send).wait_send()
            whole = pltpu.make_async_remote_copy(tok_v, tok_v, ks.at[0], kr.at[0], **to("fsdp", z))
            whole.wait_send()
            for off in range(1, ntp):
                out_relay(off).wait_recv()
            for b in range(ntp):
                proj_v[b * band:(b + 1) * band, :] = edge_in[b]
            proj_out.start()
            for off in range(1, ntp):
                out_relay(off).wait_send()

    @pl.loop(jnp.minimum(last - voting - COUNT - FINISH, pieces), pieces)
    def _(p):
        finish(p)

    for off in range(1, ntp):
        cot_copy(off).wait_send()

    @pl.when(beside)
    def _():
        for off in range(1, ntp):
            edge_cot_relay(off).wait_send()
            edge_half_copy(off).wait_send()
        out_copy(z).wait_send()

    for shard in range(n):
        for send, recv, target, ok in ((wrs, wrr, z + 1, shard <= z), (wls, wlr, z - 1, shard >= z)):
            @pl.when(inner & ok & (target > 0) & (target < n - 1))
            def _():
                line_sent(shard, send).wait_send()

    for flow in flows:
        _, _, _, way, depth = flow
        for k in range(n):
            @pl.when((depth > 0) & ((k - z) * way > 0))
            def _():
                sums_sent(flow, k).wait_send()

    for stage in range(2):
        buf, send, recv = ((ones, vs, vr), (pairs, ts, tr))[stage]
        for off in range(1, max(sizes)):
            if off < sizes[stage]:
                pltpu.make_async_remote_copy(
                    buf.at[:, 0], buf.at[:, 0], send.at[off - 1], recv.at[0, 0], **to("rep", me)).wait_send()
    pltpu.make_async_copy(grad_v, grad_v, ds.at[0]).wait()
    pltpu.make_async_copy(upd_v, upd_v, us.at[0]).wait()

    proj_out.wait()


def shards(n, nrep, ntp, tokens, cotangent, weight, momentum):
    held, half = tokens.shape
    rows, cols = weight.shape[0], weight.shape[0] * n
    width = min(WIDTH, half)
    pieces = half // width
    low = max(r for r in range(1, nrep + 1) if nrep % r == 0 and r * r <= nrep)
    chunks = max(1, min(4, half // (nrep * LANES)))
    most = max(low, nrep // low)
    scale = 1.0 / math.sqrt(held * n)
    dma = pltpu.SemaphoreType.DMA
    split = 2 if width % (2 * LANES) == 0 else 1
    hbm = pl.BlockSpec(memory_space=pltpu.HBM)
    place = pl.BlockSpec(memory_space=pl.ANY)
    given = [pltpu.with_memory_space_constraint(a, pltpu.HBM) for a in (tokens, cotangent, weight, momentum)]
    projected, update, gradient = pl.pallas_call(
        functools.partial(step, (n, nrep, ntp, pieces, width, rows, low, chunks), scale),
        out_shape=(
            jax.ShapeDtypeStruct((held, cols), BF16),
            jax.ShapeDtypeStruct((rows, half), BF16),
            jax.ShapeDtypeStruct((rows, half), BF16),
        ),
        in_specs=[hbm] * 4,
        out_specs=(place,) * 3,
        scratch_shapes=[
            pltpu.VMEM((held, half), BF16),
            pltpu.VMEM((rows, half), BF16),
            pltpu.VMEM((pieces, cols, width), BF16),
            pltpu.VMEM((pieces, cols, width), BF16),
            pltpu.VMEM((pieces, cols, width), BF16),
            pltpu.VMEM((cols, half), BF16),
            pltpu.VMEM((ntp,) + cotangent.shape, BF16),
            pltpu.VMEM((ntp,) + cotangent.shape, BF16),
            pltpu.VMEM((cols, held), BF16),
            pltpu.VMEM((cols, held), BF16),
            pltpu.VMEM((pieces, held, width), BF16),
            pltpu.VMEM((ntp, held, cols), F32),
            pltpu.VMEM((held, cols), F32),
            pltpu.VMEM((ntp, held // ntp, cols), F32),
            pltpu.VMEM((held // ntp, cols), BF16),
            pltpu.VMEM((ntp, held // ntp, cols), BF16),
            pltpu.VMEM((held, cols), BF16),
            pltpu.VMEM((pieces, rows, width), BF16),
            pltpu.VMEM((pieces, rows, width), BF16),
            pltpu.VMEM((pieces * split, most, rows, width // split), BF16),
            pltpu.VMEM((pieces * split, most, rows, width // split), BF16),
        ]
        + [dma((5,))]
        + [dma((max(1, ntp - 1),))] * 2
        + [dma((1,))] * 2
        + [dma((max(1, ntp - 1),))] * 2
        + [dma((1,)), dma((pieces,))]
        + [dma((n,)), dma((pieces, n - 2))] * 2
        + [dma((n,)), dma((n, chunks))] * 2
        + [dma((2, max(1, most - 1))), dma((n, nrep)), dma((2, most * most))]
        + [dma((max(1, ntp - 1),))] * 4
        + [dma((1,))] * 2
        + [dma((max(1, ntp - 1),))] * 2
        + [dma((max(1, most - 1),)), dma((pieces * split, max(1, most - 1)))] * 2
        + [dma((1,))] * 2,
        compiler_params=pltpu.CompilerParams(
            collective_id=0, has_side_effects=True, vmem_limit_bytes=44 * 1024 * 1024
        ),
    )(*given)
    renewed = BETA_TWO * momentum.astype(F32) + (1.0 - BETA_TWO) * gradient.astype(F32)[None]
    return (projected, update.astype(F32), renewed)


def solution(mesh):
    sizes = dict(mesh.shape)
    return jax.shard_map(
        functools.partial(shards, sizes["fsdp"], sizes["rep"], sizes["tp"]),
        mesh=mesh,
        in_specs=(
            P(("rep", "fsdp"), "tp"),
            P(("rep", "fsdp"), "tp"),
            P("fsdp", "tp"),
            P("rep", "fsdp", "tp"),
        ),
        out_specs=(P(("rep", "fsdp"), None), P("fsdp", "tp"), P("rep", "fsdp", "tp")),
        check_vma=False,
    )
```

```python
import functools
import math

import jax
import jax.numpy as jnp
from jax import lax
from jax.experimental import pallas as pl
from jax.experimental.pallas import tpu as pltpu
from jax.sharding import PartitionSpec as P

BETA_ONE = 0.9
BETA_TWO = 0.99
SOFT_WIDTH = 0.25
LANES = 128
WIDTH = 256
LAG = 3
HOLD = 0
BURST = 2
WLAG = 2
RELAY = 3
COUNT = 4
FINISH = 4
PROJ_STEPS = 8
MESH = pl.DeviceIdType.MESH
F32 = jnp.float32
BF16 = jnp.bfloat16


def step(dims, scale, tok, cot, wgt, mom, proj, upd, grad, *scratch):
    (n, nrep, ntp, pieces, width, rows, low, chunks) = dims
    (tok_v, mom_v, part, right_buf, left_buf, weights, cots, edge_cots, cots_t, edge_cots_t, edge_toks,
     halves, edge_half, edge_got, edge_out, edge_in, proj_v, upd_v, grad_v, ones, pairs) = scratch[:21]
    (loc, cs, cr, es, er, fs, fr, ks, kr, rs_s, rs_r, ls_s, ls_r, wrs, wrr, wls, wlr, wps, wpr, wqs,
     hs, hr, gs, gr, os, orr, qs, qr, vs, vr, ts, tr, us, ds) = scratch[21:]
    held_rows = tok.shape[0]
    z, me, t = lax.axis_index("fsdp"), lax.axis_index("rep"), lax.axis_index("tp")
    high = nrep // low
    split = ones.shape[0] // pieces
    part_width = width // split
    band = held_rows // ntp
    tp_cols = cot.shape[1]
    share = wgt.shape[1] // (nrep * chunks)
    inner = (z > 0) & (z < n - 1)
    beside = (z == 1) | (z == n - 2)
    own_rows = pl.ds(pl.multiple_of(z * rows, rows), rows)

    def to(axis, at):
        return dict(device_id={axis: at}, device_id_type=MESH)

    def cols(p):
        return pl.ds(pl.multiple_of(p * width, LANES), width)

    got = rs_r if n < 5 else ls_r
    flows = ((right_buf, rs_s, rs_r, 1, z), (left_buf, ls_s, got, -1, n - 1 - z))

    def cot_copy(off):
        return pltpu.make_async_remote_copy(
            cot, cots.at[t], cs.at[off - 1], cr.at[off - 1], **to("tp", lax.rem(t + off, ntp)))

    def edge_cot(target):
        return pltpu.make_async_remote_copy(cot, edge_cots.at[t], es.at[0], er.at[0], **to("fsdp", target))

    def edge_cot_relay(off):
        return pltpu.make_async_remote_copy(
            edge_cots.at[t], edge_cots.at[t], fs.at[off - 1], fr.at[off - 1], **to("tp", lax.rem(t + off, ntp)))

    def edge_tok(p, target):
        return pltpu.make_async_remote_copy(
            tok.at[:, cols(p)], edge_toks.at[p], ks.at[0], kr.at[p], **to("fsdp", target))

    def sum_copy(flow, p, k, sent=True):
        buf, send, recv, way, _ = flow
        slot = buf.at[p, pl.ds(pl.multiple_of(k * rows, rows), rows), :]
        hop = (k - z) * way
        return pltpu.make_async_remote_copy(
            slot, slot, send.at[k], recv.at[p, hop - 1 if sent else hop], **to("fsdp", z + way if sent else z))

    def sums_sent(flow, k):
        buf, send, recv, way, _ = flow
        slot = buf.at[:, pl.ds(pl.multiple_of(k * rows, rows), rows), :]
        return pltpu.make_async_remote_copy(slot, slot, send.at[k], recv.at[0, 0], **to("fsdp", z))

    def weight_cols(c):
        return pl.ds(pl.multiple_of((me * chunks + c) * share, LANES), share)

    def weight_slot(shard, c):
        return weights.at[pl.ds(pl.multiple_of(shard * rows, rows), rows), weight_cols(c)]

    def weight_line(own, shard, c, send, recv, target):
        slot = weight_slot(shard, c)
        source = wgt.at[:, weight_cols(c)] if own else slot
        return pltpu.make_async_remote_copy(
            source, slot, send.at[shard], recv.at[shard, c], **to("fsdp", target))

    def line_sent(shard, send):
        slot = plane_slot(shard, me)
        return pltpu.make_async_remote_copy(slot, slot, send.at[shard], wrr.at[shard, 0], **to("fsdp", z))

    mine, rest = lax.rem(me, low), me // low
    sizes = (low, high)

    def beside_me(way, off):
        if way == 0:
            return rest * low + lax.rem(mine + off, low)
        return lax.rem(rest + off, high) * low + mine

    def before_me(way, off):
        if way == 0:
            return rest * low + lax.rem(mine + low - off, low)
        return lax.rem(rest + high - off, high) * low + mine

    def plane_slot(shard, source, lo=0, hi=None):
        hi = chunks if hi is None else hi
        return weights.at[pl.ds(pl.multiple_of(shard * rows, rows), rows),
                          pl.ds(pl.multiple_of((source * chunks + lo) * share, LANES), (hi - lo) * share)]

    def plane_bytes(count):
        return weights.at[0:(n - 1) * rows, 0:count * share]

    def weight_plane(shard, way, off):
        slot = plane_slot(shard, me)
        return pltpu.make_async_remote_copy(
            slot, slot, wps.at[way, off - 1], wpr.at[shard, me], **to("rep", beside_me(way, off)))

    cut = (chunks + 1) // 2
    cuts = ((0, cut), (cut, chunks))

    def weight_relay(shard, way, off, onward):
        source = before_me(way, off)
        slot = plane_slot(shard, source, *cuts[way])
        return pltpu.make_async_remote_copy(
            slot, slot, wqs.at[way, (off - 1) * max(sizes) + onward - 1], wpr.at[shard, source],
            **to("rep", beside_me(1 - way, onward)))

    def weight_from(shard, source):
        slot = plane_slot(shard, source)
        return pltpu.make_async_remote_copy(
            slot, slot, wps.at[0, 0], wpr.at[shard, source], **to("rep", source))

    def plane_sent(sem, count):
        return pltpu.make_async_remote_copy(
            plane_bytes(count), plane_bytes(count), sem, wpr.at[0, 0], **to("rep", me))

    def half_copy(off):
        return pltpu.make_async_remote_copy(
            halves.at[t], halves.at[t], hs.at[off - 1], hr.at[off - 1], **to("tp", lax.rem(t + off, ntp)))

    def edge_half_copy(off):
        other = lax.rem(t + off, ntp)
        return pltpu.make_async_remote_copy(
            edge_half.at[pl.ds(pl.multiple_of(other * band, band), band), :], edge_got.at[t],
            gs.at[off - 1], gr.at[off - 1], **to("tp", other))

    def out_copy(target):
        return pltpu.make_async_remote_copy(edge_out, edge_in.at[t], os.at[0], orr.at[0], **to("fsdp", target))

    def out_relay(off):
        return pltpu.make_async_remote_copy(
            edge_in.at[t], edge_in.at[t], qs.at[off - 1], qr.at[off - 1], **to("tp", lax.rem(t + off, ntp)))

    def grad_out(p):
        return pltpu.make_async_copy(grad_v.at[p], grad.at[:, cols(p)], ds.at[0])

    def upd_out(p):
        return pltpu.make_async_copy(upd_v.at[p], upd.at[:, cols(p)], us.at[0])

    proj_out = pltpu.make_async_copy(proj_v, proj, loc.at[4])

    def group(stage, i):
        turn = lax.rem(i, 2) if low == high else 0
        along = turn if stage == 0 else 1 - turn
        size = sizes[stage]
        at = (1 - along) * mine + along * rest

        def peer(off):
            pos = lax.rem(at + off, size)
            return (1 - along) * (rest * low + pos) + along * (pos * low + mine)

        return size, at, peer

    def vote_copy(stage, i, off):
        _, at, peer = group(stage, i)
        slot = (ones, pairs)[stage].at[i, at]
        send, recv = ((vs, vr), (ts, tr))[stage]
        return pltpu.make_async_remote_copy(slot, slot, send.at[off - 1], recv.at[i, off - 1], **to("rep", peer(off)))

    def turned(source, target):
        for b in range(ntp):
            target[b * tp_cols:(b + 1) * tp_cols, :] = source[b].T

    def weight_step(s):
        for h in range(1, n - 1):
            for send, recv, shard, target, edge in (
                (wrs, wrr, z - h, z + 1, z - h == 0), (wls, wlr, z + h, z - 1, z + h == n - 1)):
                at = WLAG * (h - 1) + jnp.where(edge, BURST, 0)
                on = (target > 0) & (target < n - 1)
                here = inner & (shard >= 0) & (shard < n)

                @pl.when(here & (s == at))
                def _():
                    @pl.loop(0, chunks)
                    def _(c):
                        weight_line(False, shard, c, send, recv, z).wait_recv()

                        @pl.when(on)
                        def _():
                            weight_line(False, shard, c, send, recv, target).start()

                    for way in range(2):
                        for off in range(1, sizes[way]):
                            weight_plane(shard, way, off).start()

                @pl.when(here & (s == at + RELAY))
                def _():
                    for way in range(2):
                        for off in range(1, sizes[way]):
                            weight_from(shard, before_me(way, off)).wait_recv()
                            if cuts[way][0] < cuts[way][1]:
                                for onward in range(1, sizes[1 - way]):
                                    weight_relay(shard, way, off, onward).start()

    def weights_ready(shard):
        for a in range(1, low):
            for b in range(1, high):
                source = lax.rem(rest + high - b, high) * low + lax.rem(mine + low - a, low)
                weight_from(shard, source).wait_recv()

    def weights_sent():
        for way in range(2):
            for off in range(1, sizes[way]):
                plane_sent(wps.at[way, off - 1], chunks).wait_send()
                if cuts[way][0] < cuts[way][1]:
                    for onward in range(1, sizes[1 - way]):
                        plane_sent(wqs.at[way, (off - 1) * max(sizes) + onward - 1],
                                   cuts[way][1] - cuts[way][0]).wait_send()

    def token_step(s):
        @pl.when(beside & (s < pieces))
        def _():
            @pl.when(s == 0)
            def _():
                edge_cot(z).wait_recv()
                for off in range(1, ntp):
                    edge_cot_relay(off).start()
                for off in range(1, ntp):
                    edge_cot_relay(off).wait_recv()
                turned(edge_cots, edge_cots_t)

            edge_tok(s, z).wait_recv()
            total = jnp.dot(edge_cots_t[...], edge_toks[s], preferred_element_type=F32) + part[s].astype(F32)

            @pl.when(z == 1)
            def _():
                right_buf[s] = total.astype(BF16)

            @pl.when(z == n - 2)
            def _():
                left_buf[s] = total.astype(BF16)

    def sum_step(s):
        for first in (True, False):
            for j in range(n - 2, 0, -1):
                for flow in flows:
                    buf, _, _, way, depth = flow
                    p = s - LAG * (depth - 1) - HOLD * (n - 1 - depth - j)
                    k = z + way * j
                    ok = (p >= 0) & (p < pieces) & (k >= 0) & (k < n)

                    @pl.when(ok & ((depth == 1) if first else (depth > 1)))
                    def _():
                        if not first:
                            rk = pl.ds(pl.multiple_of(k * rows, rows), rows)
                            sum_copy(flow, p, k, False).wait_recv()
                            buf[p, rk, :] = (buf[p, rk, :].astype(F32) + part[p, rk, :].astype(F32)).astype(BF16)
                        sum_copy(flow, p, k).start()

    def vote(p):
        for flow in flows:
            @pl.when(flow[4] > 1)
            def _():
                sum_copy(flow, p, z, False).wait_recv()
        keep = jnp.where(beside, 0.0, 1.0).astype(F32)
        for q in range(split):
            i = p * split + q
            cut = slice(q * part_width, (q + 1) * part_width)
            at = pl.ds(pl.multiple_of(i * part_width, LANES), part_width)
            g = (part[p, own_rows, cut].astype(F32) * keep + right_buf[p, own_rows, cut].astype(F32)
                 + left_buf[p, own_rows, cut].astype(F32)) * scale
            grad_v[p, :, cut] = g.astype(BF16)
            blended = BETA_ONE * mom_v[:, at].astype(F32) + (1.0 - BETA_ONE) * g
            size, place, _ = group(0, i)
            ones[i, place] = jnp.clip(blended / SOFT_WIDTH, -1.0, 1.0).astype(BF16)
            for off in range(1, size):
                vote_copy(0, i, off).start()
        grad_out(p).start()

    def added(stage, i):
        size, place, _ = group(stage, i)
        for off in range(1, size):
            vote_copy(stage, i, off).wait_recv()
        buf = (ones, pairs)[stage]
        total = buf[i, 0].astype(F32)
        for b in range(1, size):
            total = total + buf[i, b].astype(F32)
        return total

    def count(p):
        for q in range(split):
            i = p * split + q
            total = added(0, i)
            size, place, _ = group(1, i)
            pairs[i, place] = total.astype(BF16)
            for off in range(1, size):
                vote_copy(1, i, off).start()

    def finish(p):
        for q in range(split):
            upd_v[p, :, q * part_width:(q + 1) * part_width] = jnp.clip(
                added(1, p * split + q), -1.0, 1.0).astype(BF16)
        upd_out(p).start()

    first_proj = max(BURST + WLAG * (n - 3), WLAG * (n - 2)) + RELAY + 2
    per = -(-pieces // PROJ_STEPS)
    speed = 3
    first_edge = min(first_proj, pieces - -(-pieces // speed))

    def product(p, toks):
        return lax.dot_general(
            toks, weights[:, cols(p)], (((1,), (1,)), ((), ())), preferred_element_type=F32)

    def project(s):
        @pl.when(inner & (s == first_edge))
        def _():
            for shard in range(n):
                @pl.when(shard != z)
                def _():
                    weights_ready(shard)
            halves[t] = jnp.zeros(halves.shape[1:], F32)
            edge_half[...] = jnp.zeros(edge_half.shape, F32)

        @pl.when(beside & (s >= first_edge) & (s < pieces))
        def _():
            @pl.loop(jnp.minimum(s, speed * (s - first_edge)), jnp.minimum(s + 1, speed * (s - first_edge + 1)))
            def _(p):
                edge_half[...] += product(p, edge_toks[p])

            @pl.when(s == pieces - 1)
            def _():
                for off in range(1, ntp):
                    edge_half_copy(off).start()

        @pl.when(beside & (s == pieces))
        def _():
            total = edge_half[pl.ds(pl.multiple_of(t * band, band), band), :]
            for off in range(1, ntp):
                edge_half_copy(off).wait_recv()
            for off in range(1, ntp):
                total = total + edge_got[lax.rem(t + off, ntp)]
            edge_out[...] = total.astype(BF16)

        @pl.when(beside & (s == pieces - 1 + LAG * (n - 3)))
        def _():
            @pl.when(z == 1)
            def _():
                out_copy(z - 1).start()

            @pl.when(z == n - 2)
            def _():
                out_copy(z + 1).start()

        @pl.when(inner & (s >= first_proj) & (s < first_proj + PROJ_STEPS))
        def _():
            for i in range(per):
                p = (s - first_proj) * per + i

                @pl.when(p < pieces)
                def _():
                    halves[t] += product(p, tok_v[:, cols(p)])

        @pl.when(inner & (s == first_proj + PROJ_STEPS))
        def _():
            for off in range(1, ntp):
                half_copy(off).start()

        @pl.when(inner & (s == first_proj + PROJ_STEPS + 1))
        def _():
            for off in range(1, ntp):
                half_copy(off).wait_recv()
            total = halves[0]
            for b in range(1, ntp):
                total = total + halves[b]
            proj_v[...] = total.astype(BF16)
            proj_out.start()
            for off in range(1, ntp):
                half_copy(off).wait_send()
            weights_sent()

    tok_load = pltpu.make_async_copy(tok, tok_v, loc.at[0])
    mom_load = pltpu.make_async_copy(mom.at[0], mom_v, loc.at[1])
    cot_load = pltpu.make_async_copy(cot, cots.at[t], loc.at[2])
    wgt_load = pltpu.make_async_copy(wgt, weights.at[own_rows, :], loc.at[3])
    barrier = pltpu.get_barrier_semaphore()
    for axis, at, size in (("tp", t, ntp), ("rep", me, nrep)):
        for off in range(1, size):
            pl.semaphore_signal(barrier, inc=1, **to(axis, lax.rem(at + off, size)))

    @pl.when(z > 0)
    def _():
        pl.semaphore_signal(barrier, inc=1, **to("fsdp", z - 1))

    @pl.when(z < n - 1)
    def _():
        pl.semaphore_signal(barrier, inc=1, **to("fsdp", z + 1))

    cot_load.start()
    tok_load.start()
    wgt_load.start()
    mom_load.start()
    pl.semaphore_wait(barrier, ntp + nrep - 2 + jnp.where(inner, 2, 1))

    for edge, target, send, recv in ((0, z + 1, wrs, wrr), (n - 1, z - 1, wls, wlr)):
        @pl.when(z == edge)
        def _():
            edge_cot(target).start()
            for p in range(BURST):
                edge_tok(p, target).start()

    for off in range(1, ntp):
        cot_copy(off).start()

    for send, recv, target in ((wrs, wrr, z + 1), (wls, wlr, z - 1)):
        @pl.when(inner & (target > 0) & (target < n - 1))
        def _():
            @pl.loop(0, chunks)
            def _(c):
                weight_line(True, z, c, send, recv, target).start()

    for edge, target, send, recv in ((0, z + 1, wrs, wrr), (n - 1, z - 1, wls, wlr)):
        @pl.when(z == edge)
        def _():
            @pl.loop(0, chunks)
            def _(c):
                weight_line(True, z, c, send, recv, target).start()

            @pl.loop(BURST, pieces)
            def _(p):
                edge_tok(p, target).start()

    for buf, edge in ((right_buf, 0), (left_buf, n - 1)):
        @pl.when(z == edge)
        def _():
            buf[:, edge * rows:(edge + 1) * rows, :] = jnp.zeros((pieces, rows, width), BF16)
    cot_load.wait()
    for off in range(1, ntp):
        cot_copy(off).wait_recv()
    turned(cots, cots_t)
    tok_load.wait()

    @pl.loop(0, pieces)
    def _(p):
        part[p] = jnp.dot(cots_t[...], tok_v[:, cols(p)], preferred_element_type=F32).astype(BF16)

    wgt_load.wait()
    mom_load.wait()

    deep = jnp.maximum(z, n - 1 - z)
    voting = LAG * (deep - 1) + HOLD * (n - 1 - deep)
    last = max(pieces + LAG * (n - 2), first_proj + PROJ_STEPS + 2)

    @pl.loop(0, last)
    def _(s):
        weight_step(s)
        token_step(s)
        sum_step(s)
        for work, at in ((vote, voting), (count, voting + COUNT), (finish, voting + COUNT + FINISH)):
            @pl.when((s >= at) & (s < at + pieces))
            def _():
                work(s - at)
        project(s)

    @pl.loop(jnp.minimum(last - voting - COUNT, pieces), pieces)
    def _(p):
        count(p)

    for edge, target, send, recv in ((0, z + 1, wrs, wrr), (n - 1, z - 1, wls, wlr)):
        @pl.when(z == edge)
        def _():
            out_copy(target).wait_recv()
            for off in range(1, ntp):
                out_relay(off).start()
            edge_cot(target).wait_send()

            line_sent(z, send).wait_send()
            whole = pltpu.make_async_remote_copy(tok_v, tok_v, ks.at[0], kr.at[0], **to("fsdp", z))
            whole.wait_send()
            for off in range(1, ntp):
                out_relay(off).wait_recv()
            for b in range(ntp):
                proj_v[b * band:(b + 1) * band, :] = edge_in[b]
            proj_out.start()
            for off in range(1, ntp):
                out_relay(off).wait_send()

    @pl.loop(jnp.minimum(last - voting - COUNT - FINISH, pieces), pieces)
    def _(p):
        finish(p)

    for off in range(1, ntp):
        cot_copy(off).wait_send()

    @pl.when(beside)
    def _():
        for off in range(1, ntp):
            edge_cot_relay(off).wait_send()
            edge_half_copy(off).wait_send()
        out_copy(z).wait_send()

    for shard in range(n):
        for send, recv, target, ok in ((wrs, wrr, z + 1, shard <= z), (wls, wlr, z - 1, shard >= z)):
            @pl.when(inner & ok & (target > 0) & (target < n - 1))
            def _():
                line_sent(shard, send).wait_send()

    for flow in flows:
        _, _, _, way, depth = flow
        for k in range(n):
            @pl.when((depth > 0) & ((k - z) * way > 0))
            def _():
                sums_sent(flow, k).wait_send()

    for stage in range(2):
        buf, send, recv = ((ones, vs, vr), (pairs, ts, tr))[stage]
        for off in range(1, max(sizes)):
            if off < sizes[stage]:
                pltpu.make_async_remote_copy(
                    buf.at[:, 0], buf.at[:, 0], send.at[off - 1], recv.at[0, 0], **to("rep", me)).wait_send()
    pltpu.make_async_copy(grad_v, grad_v, ds.at[0]).wait()
    pltpu.make_async_copy(upd_v, upd_v, us.at[0]).wait()

    proj_out.wait()


def shards(n, nrep, ntp, tokens, cotangent, weight, momentum):
    held, half = tokens.shape
    rows, cols = weight.shape[0], weight.shape[0] * n
    width = min(WIDTH, half)
    pieces = half // width
    low = max(r for r in range(1, nrep + 1) if nrep % r == 0 and r * r <= nrep)
    chunks = max(1, min(4, half // (nrep * LANES)))
    most = max(low, nrep // low)
    scale = 1.0 / math.sqrt(held * n)
    dma = pltpu.SemaphoreType.DMA
    split = 2 if width % (2 * LANES) == 0 else 1
    hbm = pl.BlockSpec(memory_space=pltpu.HBM)
    place = pl.BlockSpec(memory_space=pl.ANY)
    given = [pltpu.with_memory_space_constraint(a, pltpu.HBM) for a in (tokens, cotangent, weight, momentum)]
    projected, update, gradient = pl.pallas_call(
        functools.partial(step, (n, nrep, ntp, pieces, width, rows, low, chunks), scale),
        out_shape=(
            jax.ShapeDtypeStruct((held, cols), BF16),
            jax.ShapeDtypeStruct((rows, half), BF16),
            jax.ShapeDtypeStruct((rows, half), BF16),
        ),
        in_specs=[hbm] * 4,
        out_specs=(place,) * 3,
        scratch_shapes=[
            pltpu.VMEM((held, half), BF16),
            pltpu.VMEM((rows, half), BF16),
            pltpu.VMEM((pieces, cols, width), BF16),
            pltpu.VMEM((pieces, cols, width), BF16),
            pltpu.VMEM((pieces, cols, width), BF16),
            pltpu.VMEM((cols, half), BF16),
            pltpu.VMEM((ntp,) + cotangent.shape, BF16),
            pltpu.VMEM((ntp,) + cotangent.shape, BF16),
            pltpu.VMEM((cols, held), BF16),
            pltpu.VMEM((cols, held), BF16),
            pltpu.VMEM((pieces, held, width), BF16),
            pltpu.VMEM((ntp, held, cols), F32),
            pltpu.VMEM((held, cols), F32),
            pltpu.VMEM((ntp, held // ntp, cols), F32),
            pltpu.VMEM((held // ntp, cols), BF16),
            pltpu.VMEM((ntp, held // ntp, cols), BF16),
            pltpu.VMEM((held, cols), BF16),
            pltpu.VMEM((pieces, rows, width), BF16),
            pltpu.VMEM((pieces, rows, width), BF16),
            pltpu.VMEM((pieces * split, most, rows, width // split), BF16),
            pltpu.VMEM((pieces * split, most, rows, width // split), BF16),
        ]
        + [dma((5,))]
        + [dma((max(1, ntp - 1),))] * 2
        + [dma((1,))] * 2
        + [dma((max(1, ntp - 1),))] * 2
        + [dma((1,)), dma((pieces,))]
        + [dma((n,)), dma((pieces, n - 2))]
        + [dma((n,)), dma((pieces, n - 2) if n > 4 else (1,))]
        + [dma((n,)), dma((n, chunks))] * 2
        + [dma((2, max(1, most - 1))), dma((n, nrep)), dma((2, most * most))]
        + [dma((max(1, ntp - 1),))] * 4
        + [dma((1,))] * 2
        + [dma((max(1, ntp - 1),))] * 2
        + [dma((max(1, most - 1),)), dma((pieces * split, max(1, most - 1)))] * 2
        + [dma((1,))] * 2,
        compiler_params=pltpu.CompilerParams(
            collective_id=0, has_side_effects=True, vmem_limit_bytes=44 * 1024 * 1024
        ),
    )(*given)
    renewed = BETA_TWO * momentum.astype(F32) + (1.0 - BETA_TWO) * gradient.astype(F32)[None]
    return (projected, update.astype(F32), renewed)


def solution(mesh):
    sizes = dict(mesh.shape)
    return jax.shard_map(
        functools.partial(shards, sizes["fsdp"], sizes["rep"], sizes["tp"]),
        mesh=mesh,
        in_specs=(
            P(("rep", "fsdp"), "tp"),
            P(("rep", "fsdp"), "tp"),
            P("fsdp", "tp"),
            P("rep", "fsdp", "tp"),
        ),
        out_specs=(P(("rep", "fsdp"), None), P("fsdp", "tp"), P("rep", "fsdp", "tp")),
        check_vma=False,
    )
```

```python
import functools
import math

import jax
import jax.numpy as jnp
from jax import lax
from jax.experimental import pallas as pl
from jax.experimental.pallas import tpu as pltpu
from jax.sharding import PartitionSpec as P

BETA_ONE = 0.9
BETA_TWO = 0.99
SOFT_WIDTH = 0.25
LANES = 128
WIDTH = 256
LAG = 3
HOLD = 0
BURST = 2
WLAG = 2
RELAY = 3
COUNT = 4
FINISH = 4
PROJ_STEPS = 8
MESH = pl.DeviceIdType.MESH
F32 = jnp.float32
BF16 = jnp.bfloat16


def step(dims, scale, tok, cot, wgt, mom, proj, upd, new, *scratch):
    (n, nrep, ntp, pieces, width, rows, low, chunks) = dims
    (tok_v, mom_v, part, right_buf, left_buf, weights, cots, edge_cots, cots_t, edge_cots_t, edge_toks,
     halves, edge_half, edge_got, edge_out, edge_in, proj_v, upd_v, new_v, ones, pairs) = scratch[:21]
    (loc, cs, cr, es, er, fs, fr, ks, kr, rs_s, rs_r, ls_s, ls_r, wrs, wrr, wls, wlr, wps, wpr, wqs,
     hs, hr, gs, gr, os, orr, qs, qr, vs, vr, ts, tr, us, ds) = scratch[21:]
    held_rows = tok.shape[0]
    z, me, t = lax.axis_index("fsdp"), lax.axis_index("rep"), lax.axis_index("tp")
    high = nrep // low
    split = ones.shape[0] // pieces
    part_width = width // split
    band = held_rows // ntp
    tp_cols = cot.shape[1]
    share = wgt.shape[1] // (nrep * chunks)
    inner = (z > 0) & (z < n - 1)
    beside = (z == 1) | (z == n - 2)
    own_rows = pl.ds(pl.multiple_of(z * rows, rows), rows)

    def to(axis, at):
        return dict(device_id={axis: at}, device_id_type=MESH)

    def cols(p):
        return pl.ds(pl.multiple_of(p * width, LANES), width)

    got = rs_r if n < 5 else ls_r
    flows = ((right_buf, rs_s, rs_r, 1, z), (left_buf, ls_s, got, -1, n - 1 - z))

    def cot_copy(off):
        return pltpu.make_async_remote_copy(
            cot, cots.at[t], cs.at[off - 1], cr.at[off - 1], **to("tp", lax.rem(t + off, ntp)))

    def edge_cot(target):
        return pltpu.make_async_remote_copy(cot, edge_cots.at[t], es.at[0], er.at[0], **to("fsdp", target))

    def edge_cot_relay(off):
        return pltpu.make_async_remote_copy(
            edge_cots.at[t], edge_cots.at[t], fs.at[off - 1], fr.at[off - 1], **to("tp", lax.rem(t + off, ntp)))

    def edge_tok(p, target):
        return pltpu.make_async_remote_copy(
            tok.at[:, cols(p)], edge_toks.at[p], ks.at[0], kr.at[p], **to("fsdp", target))

    def sum_copy(flow, p, k, sent=True):
        buf, send, recv, way, _ = flow
        slot = buf.at[p, pl.ds(pl.multiple_of(k * rows, rows), rows), :]
        hop = (k - z) * way
        return pltpu.make_async_remote_copy(
            slot, slot, send.at[k], recv.at[p, hop - 1 if sent else hop], **to("fsdp", z + way if sent else z))

    def sums_sent(flow, k):
        buf, send, recv, way, _ = flow
        slot = buf.at[:, pl.ds(pl.multiple_of(k * rows, rows), rows), :]
        return pltpu.make_async_remote_copy(slot, slot, send.at[k], recv.at[0, 0], **to("fsdp", z))

    def weight_cols(c):
        return pl.ds(pl.multiple_of((me * chunks + c) * share, LANES), share)

    def weight_slot(shard, c):
        return weights.at[pl.ds(pl.multiple_of(shard * rows, rows), rows), weight_cols(c)]

    def weight_line(own, shard, c, send, recv, target):
        slot = weight_slot(shard, c)
        source = wgt.at[:, weight_cols(c)] if own else slot
        return pltpu.make_async_remote_copy(
            source, slot, send.at[shard], recv.at[shard, c], **to("fsdp", target))

    def line_sent(shard, send):
        slot = plane_slot(shard, me)
        return pltpu.make_async_remote_copy(slot, slot, send.at[shard], wrr.at[shard, 0], **to("fsdp", z))

    mine, rest = lax.rem(me, low), me // low
    sizes = (low, high)

    def beside_me(way, off):
        if way == 0:
            return rest * low + lax.rem(mine + off, low)
        return lax.rem(rest + off, high) * low + mine

    def before_me(way, off):
        if way == 0:
            return rest * low + lax.rem(mine + low - off, low)
        return lax.rem(rest + high - off, high) * low + mine

    def plane_slot(shard, source, lo=0, hi=None):
        hi = chunks if hi is None else hi
        return weights.at[pl.ds(pl.multiple_of(shard * rows, rows), rows),
                          pl.ds(pl.multiple_of((source * chunks + lo) * share, LANES), (hi - lo) * share)]

    def plane_bytes(count):
        return weights.at[0:(n - 1) * rows, 0:count * share]

    def weight_plane(shard, way, off):
        slot = plane_slot(shard, me)
        return pltpu.make_async_remote_copy(
            slot, slot, wps.at[way, off - 1], wpr.at[shard, me], **to("rep", beside_me(way, off)))

    cut = (chunks + 1) // 2
    cuts = ((0, cut), (cut, chunks))

    def weight_relay(shard, way, off, onward):
        source = before_me(way, off)
        slot = plane_slot(shard, source, *cuts[way])
        return pltpu.make_async_remote_copy(
            slot, slot, wqs.at[way, (off - 1) * max(sizes) + onward - 1], wpr.at[shard, source],
            **to("rep", beside_me(1 - way, onward)))

    def weight_from(shard, source):
        slot = plane_slot(shard, source)
        return pltpu.make_async_remote_copy(
            slot, slot, wps.at[0, 0], wpr.at[shard, source], **to("rep", source))

    def plane_sent(sem, count):
        return pltpu.make_async_remote_copy(
            plane_bytes(count), plane_bytes(count), sem, wpr.at[0, 0], **to("rep", me))

    def half_copy(off):
        return pltpu.make_async_remote_copy(
            halves.at[t], halves.at[t], hs.at[off - 1], hr.at[off - 1], **to("tp", lax.rem(t + off, ntp)))

    def edge_half_copy(off):
        other = lax.rem(t + off, ntp)
        return pltpu.make_async_remote_copy(
            edge_half.at[pl.ds(pl.multiple_of(other * band, band), band), :], edge_got.at[t],
            gs.at[off - 1], gr.at[off - 1], **to("tp", other))

    def out_copy(target):
        return pltpu.make_async_remote_copy(edge_out, edge_in.at[t], os.at[0], orr.at[0], **to("fsdp", target))

    def out_relay(off):
        return pltpu.make_async_remote_copy(
            edge_in.at[t], edge_in.at[t], qs.at[off - 1], qr.at[off - 1], **to("tp", lax.rem(t + off, ntp)))

    def new_out(p):
        return pltpu.make_async_copy(new_v.at[p], new.at[:, cols(p)], ds.at[0])

    def upd_out(p):
        return pltpu.make_async_copy(upd_v.at[p], upd.at[:, cols(p)], us.at[0])

    proj_out = pltpu.make_async_copy(proj_v, proj, loc.at[4])

    def group(stage, i):
        turn = lax.rem(i, 2) if low == high else 0
        along = turn if stage == 0 else 1 - turn
        size = sizes[stage]
        at = (1 - along) * mine + along * rest

        def peer(off):
            pos = lax.rem(at + off, size)
            return (1 - along) * (rest * low + pos) + along * (pos * low + mine)

        return size, at, peer

    def vote_copy(stage, i, off):
        _, at, peer = group(stage, i)
        slot = (ones, pairs)[stage].at[i, at]
        send, recv = ((vs, vr), (ts, tr))[stage]
        return pltpu.make_async_remote_copy(slot, slot, send.at[off - 1], recv.at[i, off - 1], **to("rep", peer(off)))

    def turned(source, target):
        for b in range(ntp):
            target[b * tp_cols:(b + 1) * tp_cols, :] = source[b].T

    def weight_step(s):
        for h in range(1, n - 1):
            for send, recv, shard, target, edge in (
                (wrs, wrr, z - h, z + 1, z - h == 0), (wls, wlr, z + h, z - 1, z + h == n - 1)):
                at = WLAG * (h - 1) + jnp.where(edge, BURST, 0)
                on = (target > 0) & (target < n - 1)
                here = inner & (shard >= 0) & (shard < n)

                @pl.when(here & (s == at))
                def _():
                    @pl.loop(0, chunks)
                    def _(c):
                        weight_line(False, shard, c, send, recv, z).wait_recv()

                        @pl.when(on)
                        def _():
                            weight_line(False, shard, c, send, recv, target).start()

                    for way in range(2):
                        for off in range(1, sizes[way]):
                            weight_plane(shard, way, off).start()

                @pl.when(here & (s == at + RELAY))
                def _():
                    for way in range(2):
                        for off in range(1, sizes[way]):
                            weight_from(shard, before_me(way, off)).wait_recv()
                            if cuts[way][0] < cuts[way][1]:
                                for onward in range(1, sizes[1 - way]):
                                    weight_relay(shard, way, off, onward).start()

    def weights_ready(shard):
        for a in range(1, low):
            for b in range(1, high):
                source = lax.rem(rest + high - b, high) * low + lax.rem(mine + low - a, low)
                weight_from(shard, source).wait_recv()

    def weights_sent():
        for way in range(2):
            for off in range(1, sizes[way]):
                plane_sent(wps.at[way, off - 1], chunks).wait_send()
                if cuts[way][0] < cuts[way][1]:
                    for onward in range(1, sizes[1 - way]):
                        plane_sent(wqs.at[way, (off - 1) * max(sizes) + onward - 1],
                                   cuts[way][1] - cuts[way][0]).wait_send()

    def token_step(s):
        @pl.when(beside & (s < pieces))
        def _():
            @pl.when(s == 0)
            def _():
                edge_cot(z).wait_recv()
                for off in range(1, ntp):
                    edge_cot_relay(off).start()
                for off in range(1, ntp):
                    edge_cot_relay(off).wait_recv()
                turned(edge_cots, edge_cots_t)

            edge_tok(s, z).wait_recv()
            total = jnp.dot(edge_cots_t[...], edge_toks[s], preferred_element_type=F32) + part[s].astype(F32)

            @pl.when(z == 1)
            def _():
                right_buf[s] = total.astype(BF16)

            @pl.when(z == n - 2)
            def _():
                left_buf[s] = total.astype(BF16)

    def sum_step(s):
        for first in (True, False):
            for j in range(n - 2, 0, -1):
                for flow in flows:
                    buf, _, _, way, depth = flow
                    p = s - LAG * (depth - 1) - HOLD * (n - 1 - depth - j)
                    k = z + way * j
                    ok = (p >= 0) & (p < pieces) & (k >= 0) & (k < n)

                    @pl.when(ok & ((depth == 1) if first else (depth > 1)))
                    def _():
                        if not first:
                            rk = pl.ds(pl.multiple_of(k * rows, rows), rows)
                            sum_copy(flow, p, k, False).wait_recv()
                            buf[p, rk, :] = (buf[p, rk, :].astype(F32) + part[p, rk, :].astype(F32)).astype(BF16)
                        sum_copy(flow, p, k).start()

    def vote(p):
        for flow in flows:
            @pl.when(flow[4] > 1)
            def _():
                sum_copy(flow, p, z, False).wait_recv()
        keep = jnp.where(beside, 0.0, 1.0).astype(F32)
        for q in range(split):
            i = p * split + q
            cut = slice(q * part_width, (q + 1) * part_width)
            at = pl.ds(pl.multiple_of(i * part_width, LANES), part_width)
            g = (part[p, own_rows, cut].astype(F32) * keep + right_buf[p, own_rows, cut].astype(F32)
                 + left_buf[p, own_rows, cut].astype(F32)) * scale
            held = mom_v[:, at].astype(F32)
            new_v[p, :, cut] = BETA_TWO * held + (1.0 - BETA_TWO) * g
            blended = BETA_ONE * held + (1.0 - BETA_ONE) * g
            size, place, _ = group(0, i)
            ones[i, place] = jnp.clip(blended / SOFT_WIDTH, -1.0, 1.0).astype(BF16)
            for off in range(1, size):
                vote_copy(0, i, off).start()
        new_out(p).start()

    def added(stage, i):
        size, place, _ = group(stage, i)
        for off in range(1, size):
            vote_copy(stage, i, off).wait_recv()
        buf = (ones, pairs)[stage]
        total = buf[i, 0].astype(F32)
        for b in range(1, size):
            total = total + buf[i, b].astype(F32)
        return total

    def count(p):
        for q in range(split):
            i = p * split + q
            total = added(0, i)
            size, place, _ = group(1, i)
            pairs[i, place] = total.astype(BF16)
            for off in range(1, size):
                vote_copy(1, i, off).start()

    def finish(p):
        for q in range(split):
            upd_v[p, :, q * part_width:(q + 1) * part_width] = jnp.clip(
                added(1, p * split + q), -1.0, 1.0)
        upd_out(p).start()

    first_proj = max(BURST + WLAG * (n - 3), WLAG * (n - 2)) + RELAY + 2
    per = -(-pieces // PROJ_STEPS)
    speed = 3
    first_edge = min(first_proj, pieces - -(-pieces // speed))

    def product(p, toks):
        return lax.dot_general(
            toks, weights[:, cols(p)], (((1,), (1,)), ((), ())), preferred_element_type=F32)

    def project(s):
        @pl.when(inner & (s == first_edge))
        def _():
            for shard in range(n):
                @pl.when(shard != z)
                def _():
                    weights_ready(shard)
            halves[t] = jnp.zeros(halves.shape[1:], F32)
            edge_half[...] = jnp.zeros(edge_half.shape, F32)

        @pl.when(beside & (s >= first_edge) & (s < pieces))
        def _():
            @pl.loop(jnp.minimum(s, speed * (s - first_edge)), jnp.minimum(s + 1, speed * (s - first_edge + 1)))
            def _(p):
                edge_half[...] += product(p, edge_toks[p])

            @pl.when(s == pieces - 1)
            def _():
                for off in range(1, ntp):
                    edge_half_copy(off).start()

        @pl.when(beside & (s == pieces))
        def _():
            total = edge_half[pl.ds(pl.multiple_of(t * band, band), band), :]
            for off in range(1, ntp):
                edge_half_copy(off).wait_recv()
            for off in range(1, ntp):
                total = total + edge_got[lax.rem(t + off, ntp)]
            edge_out[...] = total.astype(BF16)

        @pl.when(beside & (s == pieces - 1 + LAG * (n - 3)))
        def _():
            @pl.when(z == 1)
            def _():
                out_copy(z - 1).start()

            @pl.when(z == n - 2)
            def _():
                out_copy(z + 1).start()

        @pl.when(inner & (s >= first_proj) & (s < first_proj + PROJ_STEPS))
        def _():
            for i in range(per):
                p = (s - first_proj) * per + i

                @pl.when(p < pieces)
                def _():
                    halves[t] += product(p, tok_v[:, cols(p)])

        @pl.when(inner & (s == first_proj + PROJ_STEPS))
        def _():
            for off in range(1, ntp):
                half_copy(off).start()

        @pl.when(inner & (s == first_proj + PROJ_STEPS + 1))
        def _():
            for off in range(1, ntp):
                half_copy(off).wait_recv()
            total = halves[0]
            for b in range(1, ntp):
                total = total + halves[b]
            proj_v[...] = total.astype(BF16)
            proj_out.start()
            for off in range(1, ntp):
                half_copy(off).wait_send()
            weights_sent()

    tok_load = pltpu.make_async_copy(tok, tok_v, loc.at[0])
    mom_load = pltpu.make_async_copy(mom.at[0], mom_v, loc.at[1])
    cot_load = pltpu.make_async_copy(cot, cots.at[t], loc.at[2])
    wgt_load = pltpu.make_async_copy(wgt, weights.at[own_rows, :], loc.at[3])
    barrier = pltpu.get_barrier_semaphore()
    for axis, at, size in (("tp", t, ntp), ("rep", me, nrep)):
        for off in range(1, size):
            pl.semaphore_signal(barrier, inc=1, **to(axis, lax.rem(at + off, size)))

    @pl.when(z > 0)
    def _():
        pl.semaphore_signal(barrier, inc=1, **to("fsdp", z - 1))

    @pl.when(z < n - 1)
    def _():
        pl.semaphore_signal(barrier, inc=1, **to("fsdp", z + 1))

    cot_load.start()
    tok_load.start()
    wgt_load.start()
    mom_load.start()
    pl.semaphore_wait(barrier, ntp + nrep - 2 + jnp.where(inner, 2, 1))

    for edge, target, send, recv in ((0, z + 1, wrs, wrr), (n - 1, z - 1, wls, wlr)):
        @pl.when(z == edge)
        def _():
            edge_cot(target).start()
            for p in range(BURST):
                edge_tok(p, target).start()

    for off in range(1, ntp):
        cot_copy(off).start()

    for send, recv, target in ((wrs, wrr, z + 1), (wls, wlr, z - 1)):
        @pl.when(inner & (target > 0) & (target < n - 1))
        def _():
            @pl.loop(0, chunks)
            def _(c):
                weight_line(True, z, c, send, recv, target).start()

    for edge, target, send, recv in ((0, z + 1, wrs, wrr), (n - 1, z - 1, wls, wlr)):
        @pl.when(z == edge)
        def _():
            @pl.loop(0, chunks)
            def _(c):
                weight_line(True, z, c, send, recv, target).start()

            @pl.loop(BURST, pieces)
            def _(p):
                edge_tok(p, target).start()

    for buf, edge in ((right_buf, 0), (left_buf, n - 1)):
        @pl.when(z == edge)
        def _():
            buf[:, edge * rows:(edge + 1) * rows, :] = jnp.zeros((pieces, rows, width), BF16)
    cot_load.wait()
    for off in range(1, ntp):
        cot_copy(off).wait_recv()
    turned(cots, cots_t)
    tok_load.wait()

    @pl.loop(0, pieces)
    def _(p):
        part[p] = jnp.dot(cots_t[...], tok_v[:, cols(p)], preferred_element_type=F32).astype(BF16)

    wgt_load.wait()
    mom_load.wait()

    deep = jnp.maximum(z, n - 1 - z)
    voting = LAG * (deep - 1) + HOLD * (n - 1 - deep)
    last = max(pieces + LAG * (n - 2), first_proj + PROJ_STEPS + 2)

    @pl.loop(0, last)
    def _(s):
        weight_step(s)
        token_step(s)
        sum_step(s)
        for work, at in ((vote, voting), (count, voting + COUNT), (finish, voting + COUNT + FINISH)):
            @pl.when((s >= at) & (s < at + pieces))
            def _():
                work(s - at)
        project(s)

    @pl.loop(jnp.minimum(last - voting - COUNT, pieces), pieces)
    def _(p):
        count(p)

    for edge, target, send, recv in ((0, z + 1, wrs, wrr), (n - 1, z - 1, wls, wlr)):
        @pl.when(z == edge)
        def _():
            out_copy(target).wait_recv()
            for off in range(1, ntp):
                out_relay(off).start()
            edge_cot(target).wait_send()

            line_sent(z, send).wait_send()
            whole = pltpu.make_async_remote_copy(tok_v, tok_v, ks.at[0], kr.at[0], **to("fsdp", z))
            whole.wait_send()
            for off in range(1, ntp):
                out_relay(off).wait_recv()
            for b in range(ntp):
                proj_v[b * band:(b + 1) * band, :] = edge_in[b]
            proj_out.start()
            for off in range(1, ntp):
                out_relay(off).wait_send()

    @pl.loop(jnp.minimum(last - voting - COUNT - FINISH, pieces), pieces)
    def _(p):
        finish(p)

    for off in range(1, ntp):
        cot_copy(off).wait_send()

    @pl.when(beside)
    def _():
        for off in range(1, ntp):
            edge_cot_relay(off).wait_send()
            edge_half_copy(off).wait_send()
        out_copy(z).wait_send()

    for shard in range(n):
        for send, recv, target, ok in ((wrs, wrr, z + 1, shard <= z), (wls, wlr, z - 1, shard >= z)):
            @pl.when(inner & ok & (target > 0) & (target < n - 1))
            def _():
                line_sent(shard, send).wait_send()

    for flow in flows:
        _, _, _, way, depth = flow
        for k in range(n):
            @pl.when((depth > 0) & ((k - z) * way > 0))
            def _():
                sums_sent(flow, k).wait_send()

    for stage in range(2):
        buf, send, recv = ((ones, vs, vr), (pairs, ts, tr))[stage]
        for off in range(1, max(sizes)):
            if off < sizes[stage]:
                pltpu.make_async_remote_copy(
                    buf.at[:, 0], buf.at[:, 0], send.at[off - 1], recv.at[0, 0], **to("rep", me)).wait_send()
    pltpu.make_async_copy(new_v, new_v, ds.at[0]).wait()
    pltpu.make_async_copy(upd_v, upd_v, us.at[0]).wait()

    proj_out.wait()


def settle(proj, upd, new, proj_to, upd_to, mom_to, sems):
    copies = [pltpu.make_async_copy(source, target, sems.at[i]) for i, (source, target) in enumerate(
        ((upd, upd_to), (new, mom_to.at[0]), (proj, proj_to)))]
    for copy in copies:
        copy.start()
    for copy in copies:
        copy.wait()


def shards(n, nrep, ntp, tokens, cotangent, weight, momentum):
    held, half = tokens.shape
    rows, cols = weight.shape[0], weight.shape[0] * n
    width = min(WIDTH, half)
    pieces = half // width
    low = max(r for r in range(1, nrep + 1) if nrep % r == 0 and r * r <= nrep)
    chunks = max(1, min(4, half // (nrep * LANES)))
    most = max(low, nrep // low)
    scale = 1.0 / math.sqrt(held * n)
    dma = pltpu.SemaphoreType.DMA
    split = 2 if width % (2 * LANES) == 0 else 1
    hbm = pl.BlockSpec(memory_space=pltpu.HBM)
    place = pl.BlockSpec(memory_space=pl.ANY)
    given = [pltpu.with_memory_space_constraint(a, pltpu.HBM) for a in (tokens, cotangent, weight, momentum)]
    projected, update, renewed = pl.pallas_call(
        functools.partial(step, (n, nrep, ntp, pieces, width, rows, low, chunks), scale),
        out_shape=(
            jax.ShapeDtypeStruct((held, cols), BF16),
            jax.ShapeDtypeStruct((rows, half), F32),
            jax.ShapeDtypeStruct((rows, half), F32),
        ),
        in_specs=[hbm] * 4,
        out_specs=(place,) * 3,
        scratch_shapes=[
            pltpu.VMEM((held, half), BF16),
            pltpu.VMEM((rows, half), BF16),
            pltpu.VMEM((pieces, cols, width), BF16),
            pltpu.VMEM((pieces, cols, width), BF16),
            pltpu.VMEM((pieces, cols, width), BF16),
            pltpu.VMEM((cols, half), BF16),
            pltpu.VMEM((ntp,) + cotangent.shape, BF16),
            pltpu.VMEM((ntp,) + cotangent.shape, BF16),
            pltpu.VMEM((cols, held), BF16),
            pltpu.VMEM((cols, held), BF16),
            pltpu.VMEM((pieces, held, width), BF16),
            pltpu.VMEM((ntp, held, cols), F32),
            pltpu.VMEM((held, cols), F32),
            pltpu.VMEM((ntp, held // ntp, cols), F32),
            pltpu.VMEM((held // ntp, cols), BF16),
            pltpu.VMEM((ntp, held // ntp, cols), BF16),
            pltpu.VMEM((held, cols), BF16),
            pltpu.VMEM((pieces, rows, width), F32),
            pltpu.VMEM((pieces, rows, width), F32),
            pltpu.VMEM((pieces * split, most, rows, width // split), BF16),
            pltpu.VMEM((pieces * split, most, rows, width // split), BF16),
        ]
        + [dma((5,))]
        + [dma((max(1, ntp - 1),))] * 2
        + [dma((1,))] * 2
        + [dma((max(1, ntp - 1),))] * 2
        + [dma((1,)), dma((pieces,))]
        + [dma((n,)), dma((pieces, n - 2))]
        + [dma((n,)), dma((pieces, n - 2) if n > 4 else (1,))]
        + [dma((n,)), dma((n, chunks))] * 2
        + [dma((2, max(1, most - 1))), dma((n, nrep)), dma((2, most * most))]
        + [dma((max(1, ntp - 1),))] * 4
        + [dma((1,))] * 2
        + [dma((max(1, ntp - 1),))] * 2
        + [dma((max(1, most - 1),)), dma((pieces * split, max(1, most - 1)))] * 2
        + [dma((1,))] * 2,
        compiler_params=pltpu.CompilerParams(
            collective_id=0, has_side_effects=True, vmem_limit_bytes=44 * 1024 * 1024
        ),
    )(*given)
    return pl.pallas_call(
        settle,
        out_shape=(
            jax.ShapeDtypeStruct((held, cols), BF16),
            jax.ShapeDtypeStruct((rows, half), F32),
            jax.ShapeDtypeStruct((1, rows, half), F32),
        ),
        in_specs=[place] * 3,
        out_specs=(hbm,) * 3,
        scratch_shapes=[dma((3,))],
        compiler_params=pltpu.CompilerParams(vmem_limit_bytes=4 * 1024 * 1024),
    )(projected, update, renewed)


def solution(mesh):
    sizes = dict(mesh.shape)
    return jax.shard_map(
        functools.partial(shards, sizes["fsdp"], sizes["rep"], sizes["tp"]),
        mesh=mesh,
        in_specs=(
            P(("rep", "fsdp"), "tp"),
            P(("rep", "fsdp"), "tp"),
            P("fsdp", "tp"),
            P("rep", "fsdp", "tp"),
        ),
        out_specs=(P(("rep", "fsdp"), None), P("fsdp", "tp"), P("rep", "fsdp", "tp")),
        check_vma=False,
    )
```

```python
import functools
import math

import jax
import jax.numpy as jnp
from jax import lax
from jax.experimental import pallas as pl
from jax.experimental.pallas import tpu as pltpu
from jax.sharding import PartitionSpec as P

BETA_ONE = 0.9
BETA_TWO = 0.99
SOFT_WIDTH = 0.25
LANES = 128
WIDTH = 256
LAG = 3
HOLD = 0
BURST = 2
WLAG = 2
RELAY = 3
COUNT = 4
FINISH = 4
PROJ_STEPS = 8
CHUNKS = 2
STRIPS = 1
MESH = pl.DeviceIdType.MESH
F32 = jnp.float32
BF16 = jnp.bfloat16


def step(dims, scale, tok, cot, wgt, mom, proj, upd, new, *scratch):
    (n, nrep, ntp, pieces, width, rows, low, chunks) = dims
    (tok_v, mom_v, part, right_buf, left_buf, weights, cots, edge_cots, cots_t, edge_cots_t, edge_toks,
     halves, edge_half, edge_got, edge_out, edge_in, proj_v, upd_v, new_v, ones, pairs) = scratch[:21]
    (loc, cs, cr, es, er, fs, fr, ks, kr, rs_s, rs_r, ls_s, ls_r, wrs, wrr, wls, wlr, wps, wpr, wqs,
     hs, hr, gs, gr, os, orr, qs, qr, vs, vr, ts, tr, us, ds) = scratch[21:]
    held_rows = tok.shape[0]
    z, me, t = lax.axis_index("fsdp"), lax.axis_index("rep"), lax.axis_index("tp")
    high = nrep // low
    split = ones.shape[0] // pieces
    part_width = width // split
    band = held_rows // ntp
    tp_cols = cot.shape[1]
    share = wgt.shape[1] // (nrep * chunks)
    inner = (z > 0) & (z < n - 1)
    beside = (z == 1) | (z == n - 2)
    own_rows = pl.ds(pl.multiple_of(z * rows, rows), rows)

    def to(axis, at):
        return dict(device_id={axis: at}, device_id_type=MESH)

    def cols(p):
        return pl.ds(pl.multiple_of(p * width, LANES), width)

    got = rs_r if n < 5 else ls_r
    flows = ((right_buf, rs_s, rs_r, 1, z), (left_buf, ls_s, got, -1, n - 1 - z))

    def cot_copy(off):
        return pltpu.make_async_remote_copy(
            cot, cots.at[t], cs.at[off - 1], cr.at[off - 1], **to("tp", lax.rem(t + off, ntp)))

    def edge_cot(target):
        return pltpu.make_async_remote_copy(cot, edge_cots.at[t], es.at[0], er.at[0], **to("fsdp", target))

    def edge_cot_relay(off):
        return pltpu.make_async_remote_copy(
            edge_cots.at[t], edge_cots.at[t], fs.at[off - 1], fr.at[off - 1], **to("tp", lax.rem(t + off, ntp)))

    def edge_tok(p, target):
        return pltpu.make_async_remote_copy(
            tok.at[:, cols(p)], edge_toks.at[p], ks.at[0], kr.at[p], **to("fsdp", target))

    def sum_copy(flow, p, k, sent=True):
        buf, send, recv, way, _ = flow
        slot = buf.at[p, pl.ds(pl.multiple_of(k * rows, rows), rows), :]
        hop = (k - z) * way
        return pltpu.make_async_remote_copy(
            slot, slot, send.at[k], recv.at[p, hop - 1 if sent else hop], **to("fsdp", z + way if sent else z))

    def sums_sent(flow, k):
        buf, send, recv, way, _ = flow
        slot = buf.at[:, pl.ds(pl.multiple_of(k * rows, rows), rows), :]
        return pltpu.make_async_remote_copy(slot, slot, send.at[k], recv.at[0, 0], **to("fsdp", z))

    def weight_cols(c):
        return pl.ds(pl.multiple_of((me * chunks + c) * share, LANES), share)

    def weight_slot(shard, c):
        return weights.at[pl.ds(pl.multiple_of(shard * rows, rows), rows), weight_cols(c)]

    def weight_line(own, shard, c, send, recv, target):
        slot = weight_slot(shard, c)
        source = wgt.at[:, weight_cols(c)] if own else slot
        return pltpu.make_async_remote_copy(
            source, slot, send.at[shard], recv.at[shard, c], **to("fsdp", target))

    def line_sent(shard, send):
        slot = plane_slot(shard, me)
        return pltpu.make_async_remote_copy(slot, slot, send.at[shard], wrr.at[shard, 0], **to("fsdp", z))

    mine, rest = lax.rem(me, low), me // low
    sizes = (low, high)

    def beside_me(way, off):
        if way == 0:
            return rest * low + lax.rem(mine + off, low)
        return lax.rem(rest + off, high) * low + mine

    def before_me(way, off):
        if way == 0:
            return rest * low + lax.rem(mine + low - off, low)
        return lax.rem(rest + high - off, high) * low + mine

    def plane_slot(shard, source, lo=0, hi=None):
        hi = chunks if hi is None else hi
        return weights.at[pl.ds(pl.multiple_of(shard * rows, rows), rows),
                          pl.ds(pl.multiple_of((source * chunks + lo) * share, LANES), (hi - lo) * share)]

    def plane_bytes(count):
        return weights.at[0:(n - 1) * rows, 0:count * share]

    def weight_plane(shard, way, off):
        slot = plane_slot(shard, me)
        return pltpu.make_async_remote_copy(
            slot, slot, wps.at[way, off - 1], wpr.at[shard, me], **to("rep", beside_me(way, off)))

    cut = (chunks + 1) // 2
    cuts = ((0, cut), (cut, chunks))

    def weight_relay(shard, way, off, onward):
        source = before_me(way, off)
        slot = plane_slot(shard, source, *cuts[way])
        return pltpu.make_async_remote_copy(
            slot, slot, wqs.at[way, (off - 1) * max(sizes) + onward - 1], wpr.at[shard, source],
            **to("rep", beside_me(1 - way, onward)))

    def weight_from(shard, source):
        slot = plane_slot(shard, source)
        return pltpu.make_async_remote_copy(
            slot, slot, wps.at[0, 0], wpr.at[shard, source], **to("rep", source))

    def plane_sent(sem, count):
        return pltpu.make_async_remote_copy(
            plane_bytes(count), plane_bytes(count), sem, wpr.at[0, 0], **to("rep", me))

    def half_copy(off):
        return pltpu.make_async_remote_copy(
            halves.at[t], halves.at[t], hs.at[off - 1], hr.at[off - 1], **to("tp", lax.rem(t + off, ntp)))

    def edge_half_copy(off):
        other = lax.rem(t + off, ntp)
        return pltpu.make_async_remote_copy(
            edge_half.at[pl.ds(pl.multiple_of(other * band, band), band), :], edge_got.at[t],
            gs.at[off - 1], gr.at[off - 1], **to("tp", other))

    def out_copy(target):
        return pltpu.make_async_remote_copy(edge_out, edge_in.at[t], os.at[0], orr.at[0], **to("fsdp", target))

    def out_relay(off):
        return pltpu.make_async_remote_copy(
            edge_in.at[t], edge_in.at[t], qs.at[off - 1], qr.at[off - 1], **to("tp", lax.rem(t + off, ntp)))

    def new_out(p):
        return pltpu.make_async_copy(new_v.at[p], new.at[:, cols(p)], ds.at[0])

    def upd_out(p):
        return pltpu.make_async_copy(upd_v.at[p], upd.at[:, cols(p)], us.at[0])

    proj_out = pltpu.make_async_copy(proj_v, proj, loc.at[4])

    def group(stage, i):
        turn = lax.rem(i, 2) if low == high else 0
        along = turn if stage == 0 else 1 - turn
        size = sizes[stage]
        at = (1 - along) * mine + along * rest

        def peer(off):
            pos = lax.rem(at + off, size)
            return (1 - along) * (rest * low + pos) + along * (pos * low + mine)

        return size, at, peer

    def vote_copy(stage, p, q, off):
        i = p * split + q
        _, at, peer = group(stage, i)
        slot = (ones, pairs)[stage].at[i, at]
        send, recv = ((vs, vr), (ts, tr))[stage]
        return pltpu.make_async_remote_copy(slot, slot, send.at[off - 1], recv.at[p, off - 1], **to("rep", peer(off)))

    def votes_in(stage, p):
        slots = (ones, pairs)[stage].at[pl.ds(p * split, split), 0]
        send, recv = ((vs, vr), (ts, tr))[stage]
        for off in range(1, sizes[stage]):
            pltpu.make_async_remote_copy(
                slots, slots, send.at[off - 1], recv.at[p, off - 1], **to("rep", me)).wait_recv()

    def turned(source, target):
        for b in range(ntp):
            target[b * tp_cols:(b + 1) * tp_cols, :] = source[b].T

    def weight_step(s):
        for h in range(1, n - 1):
            for send, recv, shard, target, edge in (
                (wrs, wrr, z - h, z + 1, z - h == 0), (wls, wrr, z + h, z - 1, z + h == n - 1)):
                at = WLAG * (h - 1) + jnp.where(edge, BURST, 0)
                on = (target > 0) & (target < n - 1)
                here = inner & (shard >= 0) & (shard < n)

                @pl.when(here & (s == at))
                def _():
                    @pl.loop(0, chunks)
                    def _(c):
                        weight_line(False, shard, c, send, recv, z).wait_recv()

                        @pl.when(on)
                        def _():
                            weight_line(False, shard, c, send, recv, target).start()

                    for way in range(2):
                        for off in range(1, sizes[way]):
                            weight_plane(shard, way, off).start()

                @pl.when(here & (s == at + RELAY))
                def _():
                    for way in range(2):
                        for off in range(1, sizes[way]):
                            weight_from(shard, before_me(way, off)).wait_recv()
                            if cuts[way][0] < cuts[way][1]:
                                for onward in range(1, sizes[1 - way]):
                                    weight_relay(shard, way, off, onward).start()

    def weights_ready(shard):
        for a in range(1, low):
            for b in range(1, high):
                source = lax.rem(rest + high - b, high) * low + lax.rem(mine + low - a, low)
                weight_from(shard, source).wait_recv()

    def weights_sent():
        for way in range(2):
            for off in range(1, sizes[way]):
                plane_sent(wps.at[way, off - 1], chunks).wait_send()
                if cuts[way][0] < cuts[way][1]:
                    for onward in range(1, sizes[1 - way]):
                        plane_sent(wqs.at[way, (off - 1) * max(sizes) + onward - 1],
                                   cuts[way][1] - cuts[way][0]).wait_send()

    def token_step(s):
        @pl.when(beside & (s < pieces))
        def _():
            @pl.when(s == 0)
            def _():
                edge_cot(z).wait_recv()
                for off in range(1, ntp):
                    edge_cot_relay(off).start()
                for off in range(1, ntp):
                    edge_cot_relay(off).wait_recv()
                turned(edge_cots, edge_cots_t)

            edge_tok(s, z).wait_recv()
            total = jnp.dot(edge_cots_t[...], edge_toks[s], preferred_element_type=F32) + part[s].astype(F32)

            @pl.when(z == 1)
            def _():
                right_buf[s] = total.astype(BF16)

            @pl.when(z == n - 2)
            def _():
                left_buf[s] = total.astype(BF16)

    def sum_step(s):
        for first in (True, False):
            for j in range(n - 2, 0, -1):
                for flow in flows:
                    buf, _, _, way, depth = flow
                    p = s - LAG * (depth - 1) - HOLD * (n - 1 - depth - j)
                    k = z + way * j
                    ok = (p >= 0) & (p < pieces) & (k >= 0) & (k < n)

                    @pl.when(ok & ((depth == 1) if first else (depth > 1)))
                    def _():
                        if not first:
                            rk = pl.ds(pl.multiple_of(k * rows, rows), rows)
                            sum_copy(flow, p, k, False).wait_recv()
                            buf[p, rk, :] = (buf[p, rk, :].astype(F32) + part[p, rk, :].astype(F32)).astype(BF16)
                        sum_copy(flow, p, k).start()

    def vote(p):
        for flow in flows:
            @pl.when(flow[4] > 1)
            def _():
                sum_copy(flow, p, z, False).wait_recv()
        keep = jnp.where(beside, 0.0, 1.0).astype(F32)
        for q in range(split):
            i = p * split + q
            cut = slice(q * part_width, (q + 1) * part_width)
            at = pl.ds(pl.multiple_of(i * part_width, LANES), part_width)
            g = (part[p, own_rows, cut].astype(F32) * keep + right_buf[p, own_rows, cut].astype(F32)
                 + left_buf[p, own_rows, cut].astype(F32)) * scale
            held = mom_v[:, at].astype(F32)
            new_v[p, :, cut] = BETA_TWO * held + (1.0 - BETA_TWO) * g
            blended = BETA_ONE * held + (1.0 - BETA_ONE) * g
            size, place, _ = group(0, i)
            ones[i, place] = jnp.clip(blended / SOFT_WIDTH, -1.0, 1.0).astype(BF16)
            for off in range(1, size):
                vote_copy(0, p, q, off).start()
        new_out(p).start()

    def added(stage, i):
        size, place, _ = group(stage, i)
        buf = (ones, pairs)[stage]
        total = buf[i, 0].astype(F32)
        for b in range(1, size):
            total = total + buf[i, b].astype(F32)
        return total

    def count(p):
        votes_in(0, p)
        for q in range(split):
            i = p * split + q
            total = added(0, i)
            size, place, _ = group(1, i)
            pairs[i, place] = total.astype(BF16)
            for off in range(1, size):
                vote_copy(1, p, q, off).start()

    def finish(p):
        votes_in(1, p)
        for q in range(split):
            upd_v[p, :, q * part_width:(q + 1) * part_width] = jnp.clip(
                added(1, p * split + q), -1.0, 1.0)
        upd_out(p).start()

    first_proj = max(BURST + WLAG * (n - 3), WLAG * (n - 2)) + RELAY + 2
    per = -(-pieces // PROJ_STEPS)
    speed = 3
    first_edge = min(first_proj, pieces - -(-pieces // speed))

    def product(p, toks):
        return lax.dot_general(
            toks, weights[:, cols(p)], (((1,), (1,)), ((), ())), preferred_element_type=F32)

    def project(s):
        @pl.when(inner & (s == first_edge))
        def _():
            for shard in range(n):
                @pl.when(shard != z)
                def _():
                    weights_ready(shard)
            halves[t] = jnp.zeros(halves.shape[1:], F32)
            edge_half[...] = jnp.zeros(edge_half.shape, F32)

        @pl.when(beside & (s >= first_edge) & (s < pieces))
        def _():
            @pl.loop(jnp.minimum(s, speed * (s - first_edge)), jnp.minimum(s + 1, speed * (s - first_edge + 1)))
            def _(p):
                edge_half[...] += product(p, edge_toks[p])

            @pl.when(s == pieces - 1)
            def _():
                for off in range(1, ntp):
                    edge_half_copy(off).start()

        @pl.when(beside & (s == pieces))
        def _():
            total = edge_half[pl.ds(pl.multiple_of(t * band, band), band), :]
            for off in range(1, ntp):
                edge_half_copy(off).wait_recv()
            for off in range(1, ntp):
                total = total + edge_got[lax.rem(t + off, ntp)]
            edge_out[...] = total.astype(BF16)

        @pl.when(beside & (s == pieces - 1 + LAG * (n - 3)))
        def _():
            @pl.when(z == 1)
            def _():
                out_copy(z - 1).start()

            @pl.when(z == n - 2)
            def _():
                out_copy(z + 1).start()

        @pl.when(inner & (s >= first_proj) & (s < first_proj + PROJ_STEPS))
        def _():
            for i in range(per):
                p = (s - first_proj) * per + i

                @pl.when(p < pieces)
                def _():
                    halves[t] += product(p, tok_v[:, cols(p)])

        @pl.when(inner & (s == first_proj + PROJ_STEPS))
        def _():
            for off in range(1, ntp):
                half_copy(off).start()

        @pl.when(inner & (s == first_proj + PROJ_STEPS + 1))
        def _():
            for off in range(1, ntp):
                half_copy(off).wait_recv()
            total = halves[0]
            for b in range(1, ntp):
                total = total + halves[b]
            proj_v[...] = total.astype(BF16)
            proj_out.start()
            for off in range(1, ntp):
                half_copy(off).wait_send()
            weights_sent()

    tok_load = pltpu.make_async_copy(tok, tok_v, loc.at[0])
    mom_load = pltpu.make_async_copy(mom.at[0], mom_v, loc.at[1])
    cot_load = pltpu.make_async_copy(cot, cots.at[t], loc.at[2])
    wgt_load = pltpu.make_async_copy(wgt, weights.at[own_rows, :], loc.at[3])
    barrier = pltpu.get_barrier_semaphore()
    for axis, at, size in (("tp", t, ntp), ("rep", me, nrep)):
        for off in range(1, size):
            pl.semaphore_signal(barrier, inc=1, **to(axis, lax.rem(at + off, size)))

    @pl.when(z > 0)
    def _():
        pl.semaphore_signal(barrier, inc=1, **to("fsdp", z - 1))

    @pl.when(z < n - 1)
    def _():
        pl.semaphore_signal(barrier, inc=1, **to("fsdp", z + 1))

    cot_load.start()
    tok_load.start()
    wgt_load.start()
    mom_load.start()
    pl.semaphore_wait(barrier, ntp + nrep - 2 + jnp.where(inner, 2, 1))

    for edge, target, send, recv in ((0, z + 1, wrs, wrr), (n - 1, z - 1, wls, wrr)):
        @pl.when(z == edge)
        def _():
            edge_cot(target).start()
            for p in range(BURST):
                edge_tok(p, target).start()

    for off in range(1, ntp):
        cot_copy(off).start()

    for send, recv, target in ((wrs, wrr, z + 1), (wls, wrr, z - 1)):
        @pl.when(inner & (target > 0) & (target < n - 1))
        def _():
            @pl.loop(0, chunks)
            def _(c):
                weight_line(True, z, c, send, recv, target).start()

    for edge, target, send, recv in ((0, z + 1, wrs, wrr), (n - 1, z - 1, wls, wrr)):
        @pl.when(z == edge)
        def _():
            @pl.loop(0, chunks)
            def _(c):
                weight_line(True, z, c, send, recv, target).start()

            @pl.loop(BURST, pieces)
            def _(p):
                edge_tok(p, target).start()

    for buf, edge in ((right_buf, 0), (left_buf, n - 1)):
        @pl.when(z == edge)
        def _():
            buf[:, edge * rows:(edge + 1) * rows, :] = jnp.zeros((pieces, rows, width), BF16)
    cot_load.wait()
    for off in range(1, ntp):
        cot_copy(off).wait_recv()
    turned(cots, cots_t)
    tok_load.wait()

    @pl.loop(0, pieces)
    def _(p):
        part[p] = jnp.dot(cots_t[...], tok_v[:, cols(p)], preferred_element_type=F32).astype(BF16)

    wgt_load.wait()
    mom_load.wait()

    deep = jnp.maximum(z, n - 1 - z)
    voting = LAG * (deep - 1) + HOLD * (n - 1 - deep)
    last = max(pieces + LAG * (n - 2), first_proj + PROJ_STEPS + 2)

    @pl.loop(0, last)
    def _(s):
        weight_step(s)
        token_step(s)
        sum_step(s)
        for work, at in ((vote, voting), (count, voting + COUNT), (finish, voting + COUNT + FINISH)):
            @pl.when((s >= at) & (s < at + pieces))
            def _():
                work(s - at)
        project(s)

    @pl.loop(jnp.minimum(last - voting - COUNT, pieces), pieces)
    def _(p):
        count(p)

    for edge, target, send, recv in ((0, z + 1, wrs, wrr), (n - 1, z - 1, wls, wrr)):
        @pl.when(z == edge)
        def _():
            out_copy(target).wait_recv()
            for off in range(1, ntp):
                out_relay(off).start()
            edge_cot(target).wait_send()

            line_sent(z, send).wait_send()
            whole = pltpu.make_async_remote_copy(tok_v, tok_v, ks.at[0], kr.at[0], **to("fsdp", z))
            whole.wait_send()
            for off in range(1, ntp):
                out_relay(off).wait_recv()
            for b in range(ntp):
                proj_v[b * band:(b + 1) * band, :] = edge_in[b]
            proj_out.start()
            for off in range(1, ntp):
                out_relay(off).wait_send()

    @pl.loop(jnp.minimum(last - voting - COUNT - FINISH, pieces), pieces)
    def _(p):
        finish(p)

    for off in range(1, ntp):
        cot_copy(off).wait_send()

    @pl.when(beside)
    def _():
        for off in range(1, ntp):
            edge_cot_relay(off).wait_send()
            edge_half_copy(off).wait_send()
        out_copy(z).wait_send()

    for shard in range(n):
        for send, recv, target, ok in ((wrs, wrr, z + 1, shard <= z), (wls, wrr, z - 1, shard >= z)):
            @pl.when(inner & ok & (target > 0) & (target < n - 1))
            def _():
                line_sent(shard, send).wait_send()

    for flow in flows:
        _, _, _, way, depth = flow
        for k in range(n):
            @pl.when((depth > 0) & ((k - z) * way > 0))
            def _():
                sums_sent(flow, k).wait_send()

    for stage in range(2):
        buf, send, recv = ((ones, vs, vr), (pairs, ts, tr))[stage]
        for off in range(1, max(sizes)):
            if off < sizes[stage]:
                pltpu.make_async_remote_copy(
                    buf.at[:, 0], buf.at[:, 0], send.at[off - 1], recv.at[0, 0], **to("rep", me)).wait_send()
    pltpu.make_async_copy(new_v, new_v, ds.at[0]).wait()
    pltpu.make_async_copy(upd_v, upd_v, us.at[0]).wait()

    proj_out.wait()


def settle(strips, proj, upd, new, proj_to, upd_to, mom_to, sems):
    size = upd.shape[1] // strips
    pairs = ((upd, upd_to), (new, mom_to.at[0]), (proj, proj_to))
    for b in range(strips):
        at = pl.ds(b * size, size)
        for i, (source, target) in enumerate(pairs[:2]):
            pltpu.make_async_copy(source.at[:, at], target.at[:, at], sems.at[i]).start()
    pltpu.make_async_copy(proj, proj_to, sems.at[2]).start()
    for i, (source, target) in enumerate(pairs):
        pltpu.make_async_copy(source, target, sems.at[i]).wait()


def shards(n, nrep, ntp, tokens, cotangent, weight, momentum):
    held, half = tokens.shape
    rows, cols = weight.shape[0], weight.shape[0] * n
    width = min(WIDTH, half)
    pieces = half // width
    low = max(r for r in range(1, nrep + 1) if nrep % r == 0 and r * r <= nrep)
    chunks = max(1, min(CHUNKS, half // (nrep * LANES)))
    most = max(low, nrep // low)
    scale = 1.0 / math.sqrt(held * n)
    dma = pltpu.SemaphoreType.DMA
    split = 2 if width % (2 * LANES) == 0 else 1
    hbm = pl.BlockSpec(memory_space=pltpu.HBM)
    place = pl.BlockSpec(memory_space=pl.ANY)
    given = [pltpu.with_memory_space_constraint(a, pltpu.HBM) for a in (tokens, cotangent, weight, momentum)]
    projected, update, renewed = pl.pallas_call(
        functools.partial(step, (n, nrep, ntp, pieces, width, rows, low, chunks), scale),
        out_shape=(
            jax.ShapeDtypeStruct((held, cols), BF16),
            jax.ShapeDtypeStruct((rows, half), F32),
            jax.ShapeDtypeStruct((rows, half), F32),
        ),
        in_specs=[hbm] * 4,
        out_specs=(place,) * 3,
        scratch_shapes=[
            pltpu.VMEM((held, half), BF16),
            pltpu.VMEM((rows, half), BF16),
            pltpu.VMEM((pieces, cols, width), BF16),
            pltpu.VMEM((pieces, cols, width), BF16),
            pltpu.VMEM((pieces, cols, width), BF16),
            pltpu.VMEM((cols, half), BF16),
            pltpu.VMEM((ntp,) + cotangent.shape, BF16),
            pltpu.VMEM((ntp,) + cotangent.shape, BF16),
            pltpu.VMEM((cols, held), BF16),
            pltpu.VMEM((cols, held), BF16),
            pltpu.VMEM((pieces, held, width), BF16),
            pltpu.VMEM((ntp, held, cols), F32),
            pltpu.VMEM((held, cols), F32),
            pltpu.VMEM((ntp, held // ntp, cols), F32),
            pltpu.VMEM((held // ntp, cols), BF16),
            pltpu.VMEM((ntp, held // ntp, cols), BF16),
            pltpu.VMEM((held, cols), BF16),
            pltpu.VMEM((pieces, rows, width), F32),
            pltpu.VMEM((pieces, rows, width), F32),
            pltpu.VMEM((pieces * split, most, rows, width // split), BF16),
            pltpu.VMEM((pieces * split, most, rows, width // split), BF16),
        ]
        + [dma((5,))]
        + [dma((max(1, ntp - 1),))] * 2
        + [dma((1,))] * 2
        + [dma((max(1, ntp - 1),))] * 2
        + [dma((1,)), dma((pieces,))]
        + [dma((n,)), dma((pieces, n - 2))]
        + [dma((n,)), dma((pieces, n - 2) if n > 4 else (1,))]
        + [dma((n,)), dma((n, chunks)), dma((n,)), dma((1,))]
        + [dma((2, max(1, most - 1))), dma((n, nrep)), dma((2, most * most))]
        + [dma((max(1, ntp - 1),))] * 4
        + [dma((1,))] * 2
        + [dma((max(1, ntp - 1),))] * 2
        + [dma((max(1, most - 1),)), dma((pieces, max(1, most - 1)))] * 2
        + [dma((1,))] * 2,
        compiler_params=pltpu.CompilerParams(
            collective_id=0, has_side_effects=True, vmem_limit_bytes=44 * 1024 * 1024
        ),
    )(*given)
    return pl.pallas_call(
        functools.partial(settle, math.gcd(STRIPS, half // LANES)),
        out_shape=(
            jax.ShapeDtypeStruct((held, cols), BF16),
            jax.ShapeDtypeStruct((rows, half), F32),
            jax.ShapeDtypeStruct((1, rows, half), F32),
        ),
        in_specs=[place] * 3,
        out_specs=(hbm,) * 3,
        scratch_shapes=[dma((3,))],
        compiler_params=pltpu.CompilerParams(vmem_limit_bytes=4 * 1024 * 1024),
    )(projected, update, renewed)


def solution(mesh):
    sizes = dict(mesh.shape)
    return jax.shard_map(
        functools.partial(shards, sizes["fsdp"], sizes["rep"], sizes["tp"]),
        mesh=mesh,
        in_specs=(
            P(("rep", "fsdp"), "tp"),
            P(("rep", "fsdp"), "tp"),
            P("fsdp", "tp"),
            P("rep", "fsdp", "tp"),
        ),
        out_specs=(P(("rep", "fsdp"), None), P("fsdp", "tp"), P("rep", "fsdp", "tp")),
        check_vma=False,
    )
```
